1024 devices in a mesh: dp: 32 (over x_lo, y, core), tensor: 32 (over z, x_hi).
Axes of the slice: x: 8 (x_hi: 4, x_lo: 2; x = x_hi * 2 + x_lo), y: 8, z: 8, core: 2. Of those that a mesh axis runs over, the one named last changes fastest.
Arguments:
- x_long: bfloat16 [8192, 64, 128], P('dp', None, 'tensor'), may hold values from -6 to 6
- dv_long: bfloat16 [8192, 1024], P('dp'), may hold values from -0.059814453 to 0.059814453
- x_short: bfloat16 [16384, 64, 128], P('tensor', 'dp'), may hold values from -6 to 6
- dv_short: bfloat16 [16384, 1024], P('tensor'), may hold values from -0.059814453 to 0.059814453
- long_len: int32 [32], P('dp'), may hold values from 64 to 256, as said below
- short_len: int32 [32], P('tensor'), may hold values from 128 to 512, as said below
- master: float32 [64, 128, 1024], P('dp', 'tensor'), may hold values from -0.3 to 0.3
- moment1: float32 [64, 128, 1024], P('dp', 'tensor'), may hold values from -2 to 2
- moment2: float32 [64, 128, 1024], P('dp', 'tensor'), may hold values from 0.1 to 2
Outputs:
- v_long: bfloat16 [8192, 1024], P(('dp', 'tensor'))
- new_master: float32 [64, 128, 1024], P('dp', 'tensor')
- new_moment1: float32 [64, 128, 1024], P('dp', 'tensor')
- new_moment2: float32 [64, 128, 1024], P('dp', 'tensor')
- next_weight: bfloat16 [64, 128, 1024], P(None, 'tensor')
The draws below stay inside these ranges and needn't reach their ends.
Inputs may be any that keep to these rules, and one draw needn't show every extreme that they name: `long_len`: some group has all 256 rows live; every group has at least 64 and at least one. `short_len`: some group has all 512 rows live; every group has at least 128 and at least one.
All inputs are finite; a program needn't handle non-finite values.
Results may differ from the reference program's by a relative error of at most 0.005.
Values may be sent and summed in bfloat16 or wider, within the bound.
A program may use at most 32 MiB of HBM per device.

```python
import math
import jax
import jax.numpy as jnp

D = 8192
KV = 1024
D_OUTER = 64
D_INNER = 128
ROWS_L = 256
ROWS_S = 512
LONG_GROUPS = 32
SHORT_GROUPS = 32


def draw_lengths(key, count, most):
    lowest = max(most // 4, 1)
    lengths = jax.random.randint(key, (count,), lowest, most + 1, dtype=jnp.int32)
    place = jax.random.randint(jax.random.fold_in(key, 7), (), 0, count, dtype=jnp.int32)
    return jnp.where(jnp.arange(count, dtype=jnp.int32) == place, jnp.int32(most), lengths).astype(jnp.int32)


def draw_long_len(key, part):
    return draw_lengths(jax.random.fold_in(key, 11), LONG_GROUPS, ROWS_L)


def draw_short_len(key, part):
    return draw_lengths(jax.random.fold_in(key, 13), SHORT_GROUPS, ROWS_S)


def strengthened(result, key, source, target, parts, factor):
    owner, partner = [(jnp.arange(result.shape[axis_at]) // (result.shape[axis_at] // parts)).reshape([-1 if axis == axis_at else 1 for axis in range(result.ndim)]) for axis_at in (source, target)]
    chosen = jax.random.permutation(key, parts)[partner]
    strong = (owner == chosen) | (owner == (partner + parts // 2) % parts)
    return jnp.where(strong, factor * result, result)


def block_levels(rng, extent, shards, least, largest):
    factor_of = 1.0
    for axis_at, blocks in shards:
        draws = jax.random.uniform(jax.random.fold_in(jax.random.fold_in(rng, 6), axis_at), (blocks,), jnp.float32, least / len(shards), largest / len(shards))
        factor_of = factor_of * jnp.repeat(jnp.exp(draws), extent[axis_at] // blocks).reshape((-1,) + (1,) * (len(extent) - 1 - axis_at))
    return factor_of


def centred(rng, dims, spread, most, cuts=(), kind=jnp.bfloat16):
    entries = spread * jax.random.normal(rng, dims, jnp.float32)
    if cuts:
        entries = entries * block_levels(rng, dims, cuts, -0.22, 0.18)
    return jnp.clip(entries, -most, most).astype(kind)


def bell_draw_with(own_key, dims, scale, most, cuts, heavy, kind=jnp.bfloat16):
    values = scale * jax.random.normal(own_key, dims, jnp.float32)
    if cuts:
        values = values * block_levels(own_key, dims, cuts, -0.22, 0.18)
    return jnp.clip(strengthened(values, jax.random.fold_in(own_key, 3), *heavy), -most, most).astype(kind)


def setup_inputs(seed: int = 0) -> dict:
    key_of = jax.random.split(jax.random.key(seed), 10)
    x_long = bell_draw_with(key_of[0], (ROWS_L * LONG_GROUPS, D_OUTER, D_INNER), 1.0, 6.0, ((0, 32), (2, 32)), (0, 1, 32, 2.75))
    dv_long = centred(key_of[1], (ROWS_L * LONG_GROUPS, KV), 0.01, 0.059814453, ((0, 32),))
    x_short = bell_draw_with(key_of[2], (ROWS_S * SHORT_GROUPS, D_OUTER, D_INNER), 1.0, 6.0, ((0, 32), (1, 32)), (0, 2, 32, 2.75))
    dv_short = centred(key_of[3], (ROWS_S * SHORT_GROUPS, KV), 0.01, 0.059814453, ((0, 32),))
    long_len = draw_long_len(jax.random.fold_in(key_of[9], 71), 0)
    short_len = draw_short_len(jax.random.fold_in(key_of[9], 71), 0)
    master = centred(key_of[6], (D_OUTER, D_INNER, KV), 0.05, 0.3, ((0, 32), (1, 32)), jnp.float32)
    moment1 = centred(key_of[7], (D_OUTER, D_INNER, KV), 0.3, 2.0, ((0, 32), (1, 32)), jnp.float32)
    moment2 = jnp.clip(jnp.exp(math.log(2.0) - 2.9957323 * jax.random.uniform(key_of[8], (D_OUTER, D_INNER, KV), jnp.float32) ** block_levels(key_of[8], (D_OUTER, D_INNER, KV), ((0, 32), (1, 32)), -0.2, 0.2)), 0.1, 2.0)
    return dict(x_long=x_long, dv_long=dv_long, x_short=x_short, dv_short=dv_short, long_len=long_len, short_len=short_len, master=master, moment1=moment1, moment2=moment2)


def reference(x_long, dv_long, x_short, dv_short, long_len, short_len, master, moment1, moment2):
    weight = master.astype(jnp.bfloat16)
    flat_weight = weight.reshape(D, KV)
    flat_long = x_long.reshape(ROWS_L * LONG_GROUPS, D)
    flat_short = x_short.reshape(ROWS_S * SHORT_GROUPS, D)
    rows_long = jnp.arange(ROWS_L * LONG_GROUPS, dtype=jnp.int32)
    long_live = rows_long % ROWS_L < long_len[rows_long // ROWS_L]
    rows_short = jnp.arange(ROWS_S * SHORT_GROUPS, dtype=jnp.int32)
    short_live = rows_short % ROWS_S < short_len[rows_short // ROWS_S]
    values = jnp.dot(flat_long, flat_weight, preferred_element_type=jnp.float32)
    v_long = jnp.where(long_live[:, None], values, jnp.float32(0.0)).astype(jnp.bfloat16)
    live_dv_long = jnp.where(long_live[:, None], dv_long, jnp.zeros_like(dv_long))
    live_dv_short = jnp.where(short_live[:, None], dv_short, jnp.zeros_like(dv_short))
    grad_long = jnp.dot(flat_long.T, live_dv_long, preferred_element_type=jnp.float32)
    grad_short = jnp.dot(flat_short.T, live_dv_short, preferred_element_type=jnp.float32)
    grad = (grad_long + grad_short).reshape(D_OUTER, D_INNER, KV)
    new_moment1 = 0.9 * moment1 + 0.1 * grad
    new_moment2 = 0.999 * moment2 + 0.001 * grad * grad
    first_corr = 1.0 - 0.9 ** 10
    second_corr = 1.0 - 0.999 ** 10
    update = new_moment1 / first_corr / (jnp.sqrt(new_moment2 / second_corr) + 1e-08)
    new_master = master - 0.01 * (update + 0.1 * master)
    next_weight = new_master.astype(jnp.bfloat16)
    return (v_long, new_master, new_moment1, new_moment2, next_weight)
```

```python
import jax
import jax.numpy as jnp
from jax import lax
from jax.experimental import pallas as pl
from jax.experimental.pallas import tpu as pltpu
from jax.sharding import PartitionSpec as P

MESH = pl.DeviceIdType.MESH
F32 = jnp.float32
BF16 = jnp.bfloat16

NZ, NX = 8, 4
NQ, NC = 16, 2


def contract(left, right, left_dim):
    return lax.dot_general(
        left, right, (((left_dim,), (0,)), ((), ())), preferred_element_type=F32
    )


def kernel(
    xt_ref, dvl_ref, xs_ref, dvs_ref, llen_ref, slen_ref, m_ref, m1_ref, m2_ref,
    v_out, nm_out, nm1_out, nm2_out, nw_out,
    gl, gs, vp, wown, wbuf, nown,
    rc, c1, rq, sz, rsz, rsx, vz, rvz, rvx,
    send, recv,
):
    dp = lax.axis_index("dp")
    tensor = lax.axis_index("tensor")
    q, core = dp // NC, dp % NC
    z, xh = tensor // NX, tensor % NX
    kv = v_out.shape[1]

    def at_z(k):
        return (dp, lax.rem(z + k, NZ) * NX + xh)

    def at_x(k):
        return (dp, z * NX + lax.rem(xh + k, NX))

    def at_q(k):
        return (lax.rem(q + k, NQ) * NC + core, tensor)

    other = (q * NC + (1 - core), tensor)

    barrier = pltpu.get_barrier_semaphore()

    def greet(device):
        pl.semaphore_signal(barrier, inc=1, device_id=device, device_id_type=MESH)

    lax.fori_loop(1, NZ, lambda k, c: (greet(at_z(k)), c)[1], 0)
    lax.fori_loop(1, NX, lambda k, c: (greet(at_x(k)), c)[1], 0)
    lax.fori_loop(1, NQ, lambda k, c: (greet(at_q(k)), c)[1], 0)
    greet(other)

    def remote(src, dst, slot, device):
        pltpu.make_async_remote_copy(
            src_ref=src, dst_ref=dst, send_sem=send.at[slot], recv_sem=recv.at[slot],
            device_id=device, device_id_type=MESH,
        ).start()

    def wait(sem, ref):
        pltpu.make_async_copy(ref, ref, sem).wait()

    w = jnp.concatenate([m_ref[0], m_ref[1]], axis=0).astype(BF16)
    wown[...] = w

    rows = lax.broadcasted_iota(jnp.int32, dvs_ref.shape, 0)
    dvs = jnp.where(rows < slen_ref[0], dvs_ref[...], jnp.zeros_like(dvs_ref[...]))
    g = contract(xs_ref[...], dvs, 0)
    half = g.shape[0] // 2
    g0 = g[:half].reshape(half // 8, 8, kv)
    g1 = g[half:].reshape(half // 8, 8, kv)
    low = lax.broadcasted_iota(jnp.int32, g0.shape, 1) < 4
    even = jnp.where(low, g0, pltpu.roll(g1, 4, 1)).astype(BF16)
    odd = jnp.where(low, pltpu.roll(g0, 4, 1), g1).astype(BF16)
    gs[:, 0] = even
    gs[:, 1] = odd

    rows = lax.broadcasted_iota(jnp.int32, dvl_ref.shape, 0)
    dvl = jnp.where(rows < llen_ref[0], dvl_ref[...], jnp.zeros_like(dvl_ref[...]))
    gl[...] = contract(xt_ref[...], dvl, 1).astype(BF16).reshape(gl.shape)

    pl.semaphore_wait(barrier, NZ - 1 + NX - 1 + NQ - 1 + 1)

    def start(k, c):
        to = lax.rem(z + k, NZ)
        remote(gs.at[pl.ds(2 * to, 2)], rsz.at[k - 1], 0, at_z(k))
        return c

    lax.fori_loop(1, NZ, start, 0)

    def start(k, c):
        remote(wown, wbuf.at[q, core], 1, at_q(k))
        return c

    lax.fori_loop(1, NQ, start, 0)
    wbuf[q, core] = w

    remote(gl.at[:, 1 - core], rc, 2, other)
    wait(recv.at[2], rc)

    def add(i, c):
        c1[i] = (gl[i, core].astype(F32) + rc[i].astype(F32)).astype(BF16)
        return c

    lax.fori_loop(0, NQ, add, 0)

    def start(k, c):
        remote(c1.at[lax.rem(q + k, NQ)], rq.at[k - 1], 3, at_q(k))
        return c

    lax.fori_loop(1, NQ, start, 0)

    wait(recv.at[1], rq)
    remote(wbuf.at[:, core], wbuf.at[:, core], 4, other)
    wait(recv.at[4], rc)
    weights = wbuf[...].reshape(NQ * NC * 8, kv)
    vp[...] = contract(xt_ref[...], weights, 0).astype(BF16).reshape(vp.shape)

    def start(k, c):
        to = lax.rem(z + k, NZ)
        remote(vp.at[pl.ds(2 * to, 2)], rvz.at[k - 1], 5, at_z(k))
        return c

    lax.fori_loop(1, NZ, start, 0)

    wait(recv.at[0], rsz)
    total = gs[pl.ds(2 * z, 2)].astype(F32)
    for k in range(NZ - 1):
        total += rsz[k].astype(F32)
    sz[...] = total.astype(BF16).reshape(sz.shape)

    def start(k, c):
        remote(sz.at[lax.rem(xh + k, NX)], rsx.at[k - 1], 6, at_x(k))
        return c

    lax.fori_loop(1, NX, start, 0)

    wait(recv.at[3], rq)
    grad = c1[q].astype(F32)
    for k in range(NQ - 1):
        grad += rq[k].astype(F32)

    wait(recv.at[6], rsx)
    short = sz[xh].astype(F32)
    for k in range(NX - 1):
        short += rsx[k].astype(F32)
    grad += short

    first_corr = 1.0 - 0.9**10
    second_corr = 1.0 - 0.999**10
    for a in range(2):
        ga = grad[4 * a : 4 * a + 4]
        master = m_ref[a]
        new1 = 0.9 * m1_ref[a] + 0.1 * ga
        new2 = 0.999 * m2_ref[a] + 0.001 * ga * ga
        update = new1 / first_corr / (jnp.sqrt(new2 / second_corr) + 1e-08)
        new_master = master - 0.01 * (update + 0.1 * master)
        nm_out[a] = new_master
        nm1_out[a] = new1
        nm2_out[a] = new2
        nown[a] = new_master.astype(BF16)

    def start(k, c):
        remote(nown, nw_out.at[q, core], 7, at_q(k))
        return c

    lax.fori_loop(1, NQ, start, 0)
    nw_out[q, core] = nown[...]

    wait(recv.at[5], rvz)
    total = vp[pl.ds(2 * z, 2)].astype(F32)
    for k in range(NZ - 1):
        total += rvz[k].astype(F32)
    vz[...] = total.astype(BF16).reshape(vz.shape)

    def start(k, c):
        remote(vz.at[lax.rem(xh + k, NX)], rvx.at[k - 1], 8, at_x(k))
        return c

    lax.fori_loop(1, NX, start, 0)

    wait(recv.at[7], nw_out.at[pl.ds(0, NQ - 1), core])
    remote(nw_out.at[:, core], nw_out.at[:, core], 9, other)

    wait(recv.at[8], rvx)
    values = vz[xh].astype(F32)
    for k in range(NX - 1):
        values += rvx[k].astype(F32)
    own_row = tensor * 8 + lax.broadcasted_iota(jnp.int32, values.shape, 0)
    v_out[...] = jnp.where(own_row < llen_ref[0], values, 0.0).astype(BF16)

    wait(recv.at[9], nw_out.at[:, core])

    wait(send.at[0], rsz)
    wait(send.at[1], rq)
    wait(send.at[2], rc)
    wait(send.at[3], rq)
    wait(send.at[4], rc)
    wait(send.at[5], rvz)
    wait(send.at[6], rsx)
    wait(send.at[7], nw_out.at[pl.ds(0, NQ - 1), core])
    wait(send.at[8], rvx)
    wait(send.at[9], nw_out.at[:, core])


def body(x_long, dv_long, x_short, dv_short, long_len, short_len, master, moment1, moment2):
    kv = master.shape[2]
    rows_l = x_long.shape[0]
    xt = jnp.transpose(x_long, (1, 2, 0)).reshape(-1, rows_l)
    xs = x_short.reshape(x_short.shape[0], -1)
    state = jax.ShapeDtypeStruct(master.shape, F32)
    vmem = pl.BlockSpec(memory_space=pltpu.VMEM)
    smem = pl.BlockSpec(memory_space=pltpu.SMEM)
    v, nm, nm1, nm2, nw = pl.pallas_call(
        kernel,
        out_shape=(
            jax.ShapeDtypeStruct((8, kv), BF16),
            state,
            state,
            state,
            jax.ShapeDtypeStruct((NQ, NC, 2, 4, kv), BF16),
        ),
        in_specs=[vmem] * 4 + [smem] * 2 + [vmem] * 3,
        out_specs=(vmem,) * 5,
        scratch_shapes=[
            pltpu.VMEM((NQ, NC, 8, kv), BF16),
            pltpu.VMEM((NZ * NX // 2, 2, 8, kv), BF16),
            pltpu.VMEM((NZ * NX // 2, 2, 8, kv), BF16),
            pltpu.VMEM((8, kv), BF16),
            pltpu.VMEM((NQ, NC, 8, kv), BF16),
            pltpu.VMEM((2, 4, kv), BF16),
            pltpu.VMEM((NQ, 8, kv), BF16),
            pltpu.VMEM((NQ, 8, kv), BF16),
            pltpu.VMEM((NQ - 1, 8, kv), BF16),
            pltpu.VMEM((NX, 8, kv), BF16),
            pltpu.VMEM((NZ - 1, 2, 2, 8, kv), BF16),
            pltpu.VMEM((NX - 1, 8, kv), BF16),
            pltpu.VMEM((NX, 8, kv), BF16),
            pltpu.VMEM((NZ - 1, 2, 2, 8, kv), BF16),
            pltpu.VMEM((NX - 1, 8, kv), BF16),
            pltpu.SemaphoreType.DMA((10,)),
            pltpu.SemaphoreType.DMA((10,)),
        ],
        compiler_params=pltpu.CompilerParams(collective_id=0, has_side_effects=True),
    )(xt, dv_long, xs, dv_short, long_len, short_len, master, moment1, moment2)
    return v, nm, nm1, nm2, nw.reshape(NQ * NC * 2, 4, kv)


def solution(mesh):
    placed = (
        P("dp", None, "tensor"),
        P("dp", None),
        P("tensor", "dp", None),
        P("tensor", None),
        P("dp"),
        P("tensor"),
        P("dp", "tensor", None),
        P("dp", "tensor", None),
        P("dp", "tensor", None),
    )
    return jax.shard_map(
        body,
        mesh=mesh,
        in_specs=placed,
        out_specs=(
            P(("dp", "tensor"), None),
            P("dp", "tensor", None),
            P("dp", "tensor", None),
            P("dp", "tensor", None),
            P(None, "tensor", None),
        ),
        check_vma=False,
    )
```

```python
import jax
import jax.numpy as jnp
from jax import lax
from jax.experimental import pallas as pl
from jax.experimental.pallas import tpu as pltpu
from jax.sharding import PartitionSpec as P

MESH = pl.DeviceIdType.MESH
F32 = jnp.float32
BF16 = jnp.bfloat16

NZ, NX = 8, 4
NY, NC = 8, 2
NQ = 2 * NY
W, WF, GC, GQ, N, NF, S1, V1 = 0, 1, 2, 3, 4, 5, 6, 10


def contract(left, right, left_dim):
    return lax.dot_general(
        left, right, (((left_dim,), (0,)), ((), ())), preferred_element_type=F32
    )


def far_first(i):
    return lax.rem(4 + ((i + 1) // 2) * (2 * lax.rem(i, 2) - 1) + 8, 8)


def loop(n, f):
    def step(i, c):
        f(i)
        return c

    lax.fori_loop(0, n, step, 0)


def swap_quads(even, odd):
    low = lax.broadcasted_iota(jnp.int32, even.shape, 1) < 4
    return (
        jnp.where(low, even, pltpu.roll(odd, 4, 1)),
        jnp.where(low, pltpu.roll(even, 4, 1), odd),
    )


def kernel(
    xl_hbm, dvl_hbm, xs_hbm, dvs_hbm, llen_ref, slen_ref, m_hbm, m1_hbm, m2_hbm,
    v_out, nm_out, nm1_out, nm2_out, nw_out,
    xl_ref, dvl_ref, xs_ref, dvs_ref, m_ref, m1_ref, m2_ref,
    xsf, xt, gl, gs, vp, wown, wbuf, nown,
    rc, c1, rq,
    s_rz, s_rx, s_sz, s_sx, s_rzx, s_rxz,
    v_rz, v_rx, v_sz, v_sx, v_rzx, v_rxz,
    load, send, recv, recv_w, recv_n,
):
    dp = lax.axis_index("dp")
    tensor = lax.axis_index("tensor")
    q, core = dp // NC, lax.rem(dp, NC)
    z, xh = tensor // NX, lax.rem(tensor, NX)
    xl, y = q // NY, lax.rem(q, NY)
    kv = v_out.shape[1]
    cols = kv // 2

    def to_z(k):
        return lax.rem(z + k, NZ)

    def to_x(k):
        return lax.rem(xh + k, NX)

    def at_z(k):
        return (dp, to_z(k) * NX + xh)

    def at_x(k):
        return (dp, z * NX + to_x(k))

    def at_q(p):
        return (p * NC + core, tensor)

    def step_q(i):
        far = far_first(i // 2)
        side = lax.rem(xl + 1 - lax.rem(i, 2), 2) * NY
        return side + lax.rem(y + far, NY), side + lax.rem(y - far + NY, NY)

    other = (q * NC + (1 - core), tensor)
    barrier = pltpu.get_barrier_semaphore()

    def greet(device):
        pl.semaphore_signal(barrier, inc=1, device_id=device, device_id_type=MESH)

    loop(NQ - 1, lambda i: greet(at_q(step_q(i)[0])))
    loop(NZ - 1, lambda i: greet(at_z(far_first(i))))
    loop(NX - 1, lambda i: greet(at_x(i + 1)))
    greet(other)

    loads = [
        pltpu.make_async_copy(src, dst, load.at[i])
        for i, (src, dst) in enumerate((
            (m_hbm, m_ref), (xs_hbm, xs_ref), (dvs_hbm, dvs_ref),
            (xl_hbm, xl_ref), (dvl_hbm, dvl_ref), (m1_hbm, m1_ref), (m2_hbm, m2_ref),
        ))
    ]
    for copy in loads:
        copy.start()

    def remote(src, dst, slot, device, arrival=None):
        pltpu.make_async_remote_copy(
            src_ref=src, dst_ref=dst, send_sem=send.at[slot],
            recv_sem=recv.at[slot] if arrival is None else arrival,
            device_id=device, device_id_type=MESH,
        ).start()

    def wait(sem, ref):
        pltpu.make_async_copy(ref, ref, sem).wait()

    def to_other_chips(own, gathered, slot, arrivals):
        remote(own, gathered.at[q, core], slot + 1, other)
        loop(
            NQ - 1,
            lambda i: remote(
                own, gathered.at[q, core], slot, at_q(step_q(i)[0]), arrivals.at[i]
            ),
        )

    def on_to_other_core(gathered, slot, arrivals):
        def forward(i):
            chunk = gathered.at[step_q(i)[1], core]
            wait(arrivals.at[i], chunk)
            remote(chunk, chunk, slot + 1, other)

        loop(NQ - 1, forward)
        wait(recv.at[slot + 1], gathered.at[:, 1 - core])

    def first_stage(part, rz, rx, slot):
        def along_z(i):
            k = far_first(i)
            remote(part.at[0, to_z(k)], rz.at[k - 1], slot, at_z(k))

        loop(NZ - 1, along_z)
        for k in (2, 1, 3):
            remote(part.at[1, :, to_x(k)], rx.at[k - 1], slot + 1, at_x(k))

    def second_stage(part, rz, rx, sz, sx, rzx, rxz, slot):
        wait(recv.at[slot], rz)
        total = part[0, z].astype(F32)
        for k in range(NZ - 1):
            total += rz[k].astype(F32)
        sz[...] = total.astype(BF16)
        for k in (2, 1, 3):
            remote(sz.at[to_x(k)], rzx.at[k - 1], slot + 2, at_x(k))

        wait(recv.at[slot + 1], rx)
        total = part[1, :, xh].astype(F32)
        for k in range(NX - 1):
            total += rx[k].astype(F32)
        sx[...] = total.astype(BF16)

        def along_z(i):
            k = far_first(i)
            remote(sx.at[to_z(k)], rxz.at[k - 1], slot + 3, at_z(k))

        loop(NZ - 1, along_z)

    def last_sums(sz, sx, rzx, rxz, slot):
        wait(recv.at[slot + 2], rzx)
        left = sz[xh].astype(F32)
        for k in range(NX - 1):
            left += rzx[k].astype(F32)
        wait(recv.at[slot + 3], rxz)
        right = sx[z].astype(F32)
        for k in range(NZ - 1):
            right += rxz[k].astype(F32)
        return jnp.concatenate([left, right], axis=1)

    loads[0].wait()
    w = jnp.concatenate([m_ref[0], m_ref[1]], axis=0).astype(BF16)
    wown[...] = w
    pl.semaphore_wait(barrier, NZ - 1 + NX - 1 + NQ - 1 + 1)
    to_other_chips(wown, wbuf, W, recv_w)
    wbuf[q, core] = w

    loads[1].wait()
    xsf[...] = xs_ref[...].astype(F32)
    rows = xs_ref.shape[0] // 2
    live = lax.broadcasted_iota(jnp.int32, (rows, xs_ref.shape[1]), 0) < slen_ref[0]
    x0 = jnp.where(live, xsf[pl.ds(0, rows, stride=2), :], 0.0).astype(BF16)
    x1 = jnp.where(live, xsf[pl.ds(1, rows, stride=2), :], 0.0).astype(BF16)
    loads[2].wait()
    dvs = dvs_ref[...]
    g0 = contract(x0, dvs, 0).reshape(16, 8, kv)
    g1 = contract(x1, dvs, 0).reshape(16, 8, kv)
    for s, owners in enumerate(swap_quads(g0, g1)):
        owners = owners.astype(BF16).reshape(NZ, 2, 8, kv)
        for h in range(2):
            for p in range(2):
                gs[h, :, 2 * p + s] = owners[:, p, :, h * cols : (h + 1) * cols]
    first_stage(gs, s_rz, s_rx, S1)

    loads[3].wait()
    quads = xl_ref[...].astype(F32).reshape(32, 2, 8, 128)
    blocks = swap_quads(quads[:, 0], quads[:, 1])
    x = jnp.concatenate([b.reshape(256, 128) for b in blocks], axis=1)
    live = lax.broadcasted_iota(jnp.int32, x.shape, 1) < llen_ref[0]
    x = jnp.where(live, x, 0.0).astype(BF16)
    xt[...] = x
    loads[4].wait()
    gl[...] = contract(x, dvl_ref[...], 1).astype(BF16).reshape(gl.shape)
    remote(gl.at[:, 1 - core], rc, GC, other)
    wait(recv.at[GC], rc)

    def add(i):
        c1[i] = (gl[i, core].astype(F32) + rc[i].astype(F32)).astype(BF16)

    loop(NQ, add)

    def to_owner(i):
        to = step_q(i)[0]
        remote(c1.at[to], rq.at[i], GQ, at_q(to))

    loop(NQ - 1, to_owner)

    on_to_other_core(wbuf, W, recv_w)
    values = contract(xt[...], wbuf[...].reshape(NQ * NC * 8, kv), 0).astype(BF16)
    for h in range(2):
        part = values[:, h * cols : (h + 1) * cols]
        vp[h] = part.reshape(NZ, NX, 8, cols)
    first_stage(vp, v_rz, v_rx, V1)

    second_stage(gs, s_rz, s_rx, s_sz, s_sx, s_rzx, s_rxz, S1)
    wait(recv.at[GQ], rq)
    grad = c1[q].astype(F32)
    for k in range(NQ - 1):
        grad += rq[k].astype(F32)
    grad += last_sums(s_sz, s_sx, s_rzx, s_rxz, S1)

    loads[5].wait()
    loads[6].wait()
    first_corr = 1.0 - 0.9**10
    second_corr = 1.0 - 0.999**10
    for a in range(2):
        ga = grad[4 * a : 4 * a + 4]
        master = m_ref[a]
        new1 = 0.9 * m1_ref[a] + 0.1 * ga
        new2 = 0.999 * m2_ref[a] + 0.001 * ga * ga
        update = new1 / first_corr / (jnp.sqrt(new2 / second_corr) + 1e-08)
        new_master = master - 0.01 * (update + 0.1 * master)
        nown[a] = new_master.astype(BF16)
        nm_out[a] = new_master
        nm1_out[a] = new1
        nm2_out[a] = new2
    to_other_chips(nown, nw_out, N, recv_n)
    nw_out[q, core] = nown[...]

    second_stage(vp, v_rz, v_rx, v_sz, v_sx, v_rzx, v_rxz, V1)
    on_to_other_core(nw_out, N, recv_n)
    v_out[...] = last_sums(v_sz, v_sx, v_rzx, v_rxz, V1).astype(BF16)

    wait(send.at[W], rq)
    wait(send.at[WF], rc)
    wait(send.at[GC], rc)
    wait(send.at[GQ], rq)
    wait(send.at[N], rq)
    wait(send.at[NF], rc)
    for slot, (rz, rx, rzx, rxz) in (
        (S1, (s_rz, s_rx, s_rzx, s_rxz)),
        (V1, (v_rz, v_rx, v_rzx, v_rxz)),
    ):
        wait(send.at[slot], rz)
        wait(send.at[slot + 1], rx)
        wait(send.at[slot + 2], rzx)
        wait(send.at[slot + 3], rxz)


def hand_over(*refs):
    n = len(refs) // 2
    copies = [
        pltpu.make_async_copy(refs[i], refs[n + i], refs[-1].at[i]) for i in range(n)
    ]
    for copy in copies:
        copy.start()
    for copy in copies:
        copy.wait()


def body(x_long, dv_long, x_short, dv_short, long_len, short_len, master, moment1, moment2):
    kv = master.shape[2]
    cols = kv // 2
    rows_l, outer, inner = x_long.shape
    xl = jnp.transpose(x_long, (1, 2, 0)).reshape(outer, inner, rows_l // 128, 128)
    xl = jnp.transpose(xl, (0, 2, 1, 3)).reshape(-1, 128)
    xs = x_short.reshape(-1, x_short.shape[2])
    operands = (xl, dv_long, xs, dv_short, long_len, short_len, master, moment1, moment2)
    state = jax.ShapeDtypeStruct(master.shape, F32)
    outs = (
        jax.ShapeDtypeStruct((8, kv), BF16),
        state,
        state,
        state,
        jax.ShapeDtypeStruct((NQ, NC, 2, 4, kv), BF16),
    )
    vmem = pl.BlockSpec(memory_space=pltpu.VMEM)
    hbm = pl.BlockSpec(memory_space=pl.ANY)
    smem = pl.BlockSpec(memory_space=pltpu.SMEM)
    sums = [
        pltpu.VMEM((NZ - 1, NX, 8, cols), BF16),
        pltpu.VMEM((NX - 1, NZ, 8, cols), BF16),
        pltpu.VMEM((NX, 8, cols), BF16),
        pltpu.VMEM((NZ, 8, cols), BF16),
        pltpu.VMEM((NX - 1, 8, cols), BF16),
        pltpu.VMEM((NZ - 1, 8, cols), BF16),
    ]
    results = pl.pallas_call(
        kernel,
        out_shape=tuple(pltpu.VMEM(o.shape, o.dtype) for o in outs),
        in_specs=[hbm] * 4 + [smem] * 2 + [hbm] * 3,
        out_specs=(vmem,) * 5,
        scratch_shapes=[
            pltpu.VMEM(a.shape, a.dtype) for a in operands if a.dtype != jnp.int32
        ]
        + [
            pltpu.VMEM(xs.shape, F32),
            pltpu.VMEM((outer * inner, rows_l), BF16),
            pltpu.VMEM((NQ, NC, 8, kv), BF16),
            pltpu.VMEM((2, NZ, NX, 8, cols), BF16),
            pltpu.VMEM((2, NZ, NX, 8, cols), BF16),
            pltpu.VMEM((8, kv), BF16),
            pltpu.VMEM((NQ, NC, 8, kv), BF16),
            pltpu.VMEM((2, 4, kv), BF16),
            pltpu.VMEM((NQ, 8, kv), BF16),
            pltpu.VMEM((NQ, 8, kv), BF16),
            pltpu.VMEM((NQ - 1, 8, kv), BF16),
        ]
        + sums
        + sums
        + [
            pltpu.SemaphoreType.DMA((7,)),
            pltpu.SemaphoreType.DMA((14,)),
            pltpu.SemaphoreType.DMA((14,)),
            pltpu.SemaphoreType.DMA((NQ - 1,)),
            pltpu.SemaphoreType.DMA((NQ - 1,)),
        ],
        compiler_params=pltpu.CompilerParams(collective_id=0, has_side_effects=True),
    )(*operands)
    v, nm, nm1, nm2, nw = pl.pallas_call(
        hand_over,
        out_shape=outs,
        in_specs=[vmem] * 5,
        out_specs=(hbm,) * 5,
        scratch_shapes=[pltpu.SemaphoreType.DMA((5,))],
    )(*(pltpu.with_memory_space_constraint(r, pltpu.VMEM) for r in results))
    return v, nm, nm1, nm2, nw.reshape(NQ * NC * 2, 4, kv)


def solution(mesh):
    placed = (
        P("dp", None, "tensor"),
        P("dp", None),
        P("tensor", "dp", None),
        P("tensor", None),
        P("dp"),
        P("tensor"),
        P("dp", "tensor", None),
        P("dp", "tensor", None),
        P("dp", "tensor", None),
    )
    return jax.shard_map(
        body,
        mesh=mesh,
        in_specs=placed,
        out_specs=(
            P(("dp", "tensor"), None),
            P("dp", "tensor", None),
            P("dp", "tensor", None),
            P("dp", "tensor", None),
            P(None, "tensor", None),
        ),
        check_vma=False,
    )
```

```python
import jax
import jax.numpy as jnp
from jax import lax
from jax.experimental import pallas as pl
from jax.experimental.pallas import tpu as pltpu
from jax.sharding import PartitionSpec as P

MESH = pl.DeviceIdType.MESH
F32 = jnp.float32
BF16 = jnp.bfloat16

NZ, NX = 8, 4
NY, NC = 8, 2
NQ = 2 * NY
W, WF, GC, GQ, N, NF, S1, V1 = 0, 1, 2, 3, 4, 5, 6, 10


def contract(left, right, left_dim):
    return lax.dot_general(
        left, right, (((left_dim,), (0,)), ((), ())), preferred_element_type=F32
    )


def far_first(i):
    return lax.rem(4 + ((i + 1) // 2) * (2 * lax.rem(i, 2) - 1) + 8, 8)


def loop(n, f):
    def step(i, c):
        f(i)
        return c

    lax.fori_loop(0, n, step, 0)


def swap_quads(even, odd):
    low = lax.broadcasted_iota(jnp.int32, even.shape, 1) < 4
    return (
        jnp.where(low, even, pltpu.roll(odd, 4, 1)),
        jnp.where(low, pltpu.roll(even, 4, 1), odd),
    )


def kernel(
    xl_hbm, dvl_hbm, xs_hbm, dvs_hbm, llen_ref, slen_ref, m_hbm, m1_hbm, m2_hbm,
    v_out, nm_out, nm1_out, nm2_out, nw_out,
    xl_ref, dvl_ref, xs_ref, dvs_ref, m_ref, m1_ref, m2_ref,
    xsf, xt, gl, gs, vp, wown, wbuf, nown,
    rc, c1, rq,
    s_rz, s_rx, s_sz, s_sx, s_rzx, s_rxz,
    v_rz, v_rx, v_sz, v_sx, v_rzx, v_rxz,
    load, send, recv, recv_w, recv_n,
):
    dp = lax.axis_index("dp")
    tensor = lax.axis_index("tensor")
    q, core = dp // NC, lax.rem(dp, NC)
    z, xh = tensor // NX, lax.rem(tensor, NX)
    xl, y = q // NY, lax.rem(q, NY)
    kv = v_out.shape[1]
    cols = kv // 2

    def to_z(k):
        return lax.rem(z + k, NZ)

    def to_x(k):
        return lax.rem(xh + k, NX)

    def at_z(k):
        return (dp, to_z(k) * NX + xh)

    def at_x(k):
        return (dp, z * NX + to_x(k))

    def at_q(p):
        return (p * NC + core, tensor)

    def step_q(i):
        far = far_first(i // 2)
        side = lax.rem(xl + 1 - lax.rem(i, 2), 2) * NY
        return side + lax.rem(y + far, NY), side + lax.rem(y - far + NY, NY)

    other = (q * NC + (1 - core), tensor)
    barrier = pltpu.get_barrier_semaphore()

    def greet(device):
        pl.semaphore_signal(barrier, inc=1, device_id=device, device_id_type=MESH)

    loop(NQ - 1, lambda i: greet(at_q(step_q(i)[0])))
    loop(NZ - 1, lambda i: greet(at_z(far_first(i))))
    loop(NX - 1, lambda i: greet(at_x(i + 1)))
    greet(other)

    loads = [
        pltpu.make_async_copy(src, dst, load.at[i])
        for i, (src, dst) in enumerate((
            (xs_hbm, xs_ref), (dvs_hbm, dvs_ref), (m_hbm, m_ref),
            (xl_hbm, xl_ref), (dvl_hbm, dvl_ref),
            (m1_hbm, m1_ref), (m2_hbm, m2_ref),
        ))
    ]
    for copy in loads:
        copy.start()

    def remote(src, dst, slot, device, arrival=None):
        pltpu.make_async_remote_copy(
            src_ref=src, dst_ref=dst, send_sem=send.at[slot],
            recv_sem=recv.at[slot] if arrival is None else arrival,
            device_id=device, device_id_type=MESH,
        ).start()

    def wait(sem, ref):
        pltpu.make_async_copy(ref, ref, sem).wait()

    def to_other_chips(own, gathered, slot, arrivals):
        remote(own, gathered.at[q, core], slot + 1, other)
        loop(
            NQ - 1,
            lambda i: remote(
                own, gathered.at[q, core], slot, at_q(step_q(i)[0]), arrivals.at[i]
            ),
        )

    def on_to_other_core(gathered, slot, arrivals):
        def forward(i):
            chunk = gathered.at[step_q(i)[1], core]
            wait(arrivals.at[i], chunk)
            remote(chunk, chunk, slot + 1, other)

        loop(NQ - 1, forward)

    def first_stage(part, rz, rx, slot):
        def along_z(i):
            k = far_first(i)
            remote(part.at[0, to_z(k)], rz.at[k - 1], slot, at_z(k))

        loop(NZ - 1, along_z)
        for k in (2, 1, 3):
            remote(part.at[1, :, to_x(k)], rx.at[k - 1], slot + 1, at_x(k))

    def second_stage(part, rz, rx, sz, sx, rzx, rxz, slot):
        wait(recv.at[slot], rz)
        total = part[0, z].astype(F32)
        for k in range(NZ - 1):
            total += rz[k].astype(F32)
        sz[...] = total.astype(BF16)
        for k in (2, 1, 3):
            remote(sz.at[to_x(k)], rzx.at[k - 1], slot + 2, at_x(k))

        wait(recv.at[slot + 1], rx)
        total = part[1, :, xh].astype(F32)
        for k in range(NX - 1):
            total += rx[k].astype(F32)
        sx[...] = total.astype(BF16)

        def along_z(i):
            k = far_first(i)
            remote(sx.at[to_z(k)], rxz.at[k - 1], slot + 3, at_z(k))

        loop(NZ - 1, along_z)

    def last_sums(sz, sx, rzx, rxz, slot):
        wait(recv.at[slot + 2], rzx)
        left = sz[xh].astype(F32)
        for k in range(NX - 1):
            left += rzx[k].astype(F32)
        wait(recv.at[slot + 3], rxz)
        right = sx[z].astype(F32)
        for k in range(NZ - 1):
            right += rxz[k].astype(F32)
        return jnp.concatenate([left, right], axis=1)

    loads[0].wait()
    xsf[...] = xs_ref[...].astype(F32)
    rows = xs_ref.shape[0] // 2
    live = lax.broadcasted_iota(jnp.int32, (rows, xs_ref.shape[1]), 0) < slen_ref[0]
    x0 = jnp.where(live, xsf[pl.ds(0, rows, stride=2), :], 0.0).astype(BF16)
    x1 = jnp.where(live, xsf[pl.ds(1, rows, stride=2), :], 0.0).astype(BF16)
    loads[1].wait()
    dvs = dvs_ref[...]
    g0 = contract(x0, dvs, 0).reshape(16, 8, kv)
    g1 = contract(x1, dvs, 0).reshape(16, 8, kv)
    for s, owners in enumerate(swap_quads(g0, g1)):
        owners = owners.astype(BF16).reshape(NZ, 2, 8, kv)
        for h in range(2):
            for p in range(2):
                gs[h, :, 2 * p + s] = owners[:, p, :, h * cols : (h + 1) * cols]

    loads[2].wait()
    w = jnp.concatenate([m_ref[0], m_ref[1]], axis=0).astype(BF16)
    wown[...] = w
    wbuf[q, core] = w

    loads[3].wait()
    quads = xl_ref[...].astype(F32).reshape(32, 2, 8, 128)
    blocks = swap_quads(quads[:, 0], quads[:, 1])
    x = jnp.concatenate([b.reshape(256, 128) for b in blocks], axis=1)
    live = lax.broadcasted_iota(jnp.int32, x.shape, 1) < llen_ref[0]
    x = jnp.where(live, x, 0.0).astype(BF16)
    xt[...] = x
    loads[4].wait()
    gl[...] = contract(x, dvl_ref[...], 1).astype(BF16).reshape(gl.shape)

    pl.semaphore_wait(barrier, NZ - 1 + NX - 1 + NQ - 1 + 1)
    remote(gl.at[:, 1 - core], rc, GC, other)
    to_other_chips(wown, wbuf, W, recv_w)
    first_stage(gs, s_rz, s_rx, S1)

    wait(recv.at[GC], rc)

    def add(i):
        c1[i] = (gl[i, core].astype(F32) + rc[i].astype(F32)).astype(BF16)

    loop(NQ, add)

    def to_owner(i):
        to = step_q(i)[0]
        remote(c1.at[to], rq.at[i], GQ, at_q(to))

    loop(NQ - 1, to_owner)

    on_to_other_core(wbuf, W, recv_w)
    second_stage(gs, s_rz, s_rx, s_sz, s_sx, s_rzx, s_rxz, S1)

    wait(recv.at[WF], wbuf.at[:, 1 - core])
    values = contract(xt[...], wbuf[...].reshape(NQ * NC * 8, kv), 0).astype(BF16)
    for h in range(2):
        part = values[:, h * cols : (h + 1) * cols]
        vp[h] = part.reshape(NZ, NX, 8, cols)
    first_stage(vp, v_rz, v_rx, V1)

    wait(recv.at[GQ], rq)
    grad = c1[q].astype(F32)
    for k in range(NQ - 1):
        grad += rq[k].astype(F32)
    grad += last_sums(s_sz, s_sx, s_rzx, s_rxz, S1)

    loads[5].wait()
    loads[6].wait()
    first_corr = 1.0 - 0.9**10
    second_corr = 1.0 - 0.999**10
    for a in range(2):
        ga = grad[4 * a : 4 * a + 4]
        master = m_ref[a]
        new1 = 0.9 * m1_ref[a] + 0.1 * ga
        new2 = 0.999 * m2_ref[a] + 0.001 * ga * ga
        update = new1 / first_corr / (jnp.sqrt(new2 / second_corr) + 1e-08)
        new_master = master - 0.01 * (update + 0.1 * master)
        nown[a] = new_master.astype(BF16)
        nm_out[a] = new_master
        nm1_out[a] = new1
        nm2_out[a] = new2
    to_other_chips(nown, nw_out, N, recv_n)
    nw_out[q, core] = nown[...]

    second_stage(vp, v_rz, v_rx, v_sz, v_sx, v_rzx, v_rxz, V1)
    on_to_other_core(nw_out, N, recv_n)
    v_out[...] = last_sums(v_sz, v_sx, v_rzx, v_rxz, V1).astype(BF16)
    wait(recv.at[NF], nw_out.at[:, 1 - core])

    wait(send.at[W], rq)
    wait(send.at[WF], rc)
    wait(send.at[GC], rc)
    wait(send.at[GQ], rq)
    wait(send.at[N], rq)
    wait(send.at[NF], rc)
    for slot, (rz, rx, rzx, rxz) in (
        (S1, (s_rz, s_rx, s_rzx, s_rxz)),
        (V1, (v_rz, v_rx, v_rzx, v_rxz)),
    ):
        wait(send.at[slot], rz)
        wait(send.at[slot + 1], rx)
        wait(send.at[slot + 2], rzx)
        wait(send.at[slot + 3], rxz)


def hand_over(*refs):
    n = len(refs) // 2
    copies = [
        pltpu.make_async_copy(refs[i], refs[n + i], refs[-1].at[i]) for i in range(n)
    ]
    for copy in copies:
        copy.start()
    for copy in copies:
        copy.wait()


def body(x_long, dv_long, x_short, dv_short, long_len, short_len, master, moment1, moment2):
    kv = master.shape[2]
    cols = kv // 2
    rows_l, outer, inner = x_long.shape
    xl = jnp.transpose(x_long, (1, 2, 0)).reshape(outer, inner, rows_l // 128, 128)
    xl = jnp.transpose(xl, (0, 2, 1, 3)).reshape(-1, 128)
    xs = x_short.reshape(-1, x_short.shape[2])
    operands = (xl, dv_long, xs, dv_short, long_len, short_len, master, moment1, moment2)
    state = jax.ShapeDtypeStruct(master.shape, F32)
    outs = (
        jax.ShapeDtypeStruct((8, kv), BF16),
        state,
        state,
        state,
        jax.ShapeDtypeStruct((NQ, NC, 2, 4, kv), BF16),
    )
    vmem = pl.BlockSpec(memory_space=pltpu.VMEM)
    hbm = pl.BlockSpec(memory_space=pl.ANY)
    smem = pl.BlockSpec(memory_space=pltpu.SMEM)
    sums = [
        pltpu.VMEM((NZ - 1, NX, 8, cols), BF16),
        pltpu.VMEM((NX - 1, NZ, 8, cols), BF16),
        pltpu.VMEM((NX, 8, cols), BF16),
        pltpu.VMEM((NZ, 8, cols), BF16),
        pltpu.VMEM((NX - 1, 8, cols), BF16),
        pltpu.VMEM((NZ - 1, 8, cols), BF16),
    ]
    results = pl.pallas_call(
        kernel,
        out_shape=tuple(pltpu.VMEM(o.shape, o.dtype) for o in outs),
        in_specs=[hbm] * 4 + [smem] * 2 + [hbm] * 3,
        out_specs=(vmem,) * 5,
        scratch_shapes=[
            pltpu.VMEM(a.shape, a.dtype) for a in operands if a.dtype != jnp.int32
        ]
        + [
            pltpu.VMEM(xs.shape, F32),
            pltpu.VMEM((outer * inner, rows_l), BF16),
            pltpu.VMEM((NQ, NC, 8, kv), BF16),
            pltpu.VMEM((2, NZ, NX, 8, cols), BF16),
            pltpu.VMEM((2, NZ, NX, 8, cols), BF16),
            pltpu.VMEM((8, kv), BF16),
            pltpu.VMEM((NQ, NC, 8, kv), BF16),
            pltpu.VMEM((2, 4, kv), BF16),
            pltpu.VMEM((NQ, 8, kv), BF16),
            pltpu.VMEM((NQ, 8, kv), BF16),
            pltpu.VMEM((NQ - 1, 8, kv), BF16),
        ]
        + sums
        + sums
        + [
            pltpu.SemaphoreType.DMA((7,)),
            pltpu.SemaphoreType.DMA((14,)),
            pltpu.SemaphoreType.DMA((14,)),
            pltpu.SemaphoreType.DMA((NQ - 1,)),
            pltpu.SemaphoreType.DMA((NQ - 1,)),
        ],
        compiler_params=pltpu.CompilerParams(collective_id=0, has_side_effects=True),
    )(*operands)
    v, nm, nm1, nm2, nw = pl.pallas_call(
        hand_over,
        out_shape=outs,
        in_specs=[vmem] * 5,
        out_specs=(hbm,) * 5,
        scratch_shapes=[pltpu.SemaphoreType.DMA((5,))],
    )(*(pltpu.with_memory_space_constraint(r, pltpu.VMEM) for r in results))
    return v, nm, nm1, nm2, nw.reshape(NQ * NC * 2, 4, kv)


def solution(mesh):
    placed = (
        P("dp", None, "tensor"),
        P("dp", None),
        P("tensor", "dp", None),
        P("tensor", None),
        P("dp"),
        P("tensor"),
        P("dp", "tensor", None),
        P("dp", "tensor", None),
        P("dp", "tensor", None),
    )
    return jax.shard_map(
        body,
        mesh=mesh,
        in_specs=placed,
        out_specs=(
            P(("dp", "tensor"), None),
            P("dp", "tensor", None),
            P("dp", "tensor", None),
            P("dp", "tensor", None),
            P(None, "tensor", None),
        ),
        check_vma=False,
    )
```

```python
import jax
import jax.numpy as jnp
from jax import lax
from jax.experimental import pallas as pl
from jax.experimental.pallas import tpu as pltpu
from jax.sharding import PartitionSpec as P

MESH = pl.DeviceIdType.MESH
F32 = jnp.float32
BF16 = jnp.bfloat16

NZ, NX = 8, 4
NY, NC = 8, 2
NQ = 2 * NY
W, WF, GC, GQ, N, NF, S1, V1 = 0, 1, 2, 3, 4, 5, 6, 10


def contract(left, right, left_dim):
    return lax.dot_general(
        left, right, (((left_dim,), (0,)), ((), ())), preferred_element_type=F32
    )


def far_first(i):
    return lax.rem(4 + ((i + 1) // 2) * (2 * lax.rem(i, 2) - 1) + 8, 8)


def loop(n, f):
    def step(i, c):
        f(i)
        return c

    lax.fori_loop(0, n, step, 0)


def swap_quads(even, odd):
    low = lax.broadcasted_iota(jnp.int32, even.shape, 1) < 4
    return (
        jnp.where(low, even, pltpu.roll(odd, 4, 1)),
        jnp.where(low, pltpu.roll(even, 4, 1), odd),
    )


def kernel(
    xl_hbm, dvl_hbm, xs_hbm, dvs_hbm, llen_ref, slen_ref, m_hbm, m1_hbm, m2_hbm,
    v_out, nm_out, nm1_out, nm2_out, nw_out,
    xl_ref, dvl_ref, xs_ref, dvs_ref, m_ref, m1_ref, m2_ref,
    xsf, xt, gl, gsz, gsx, vpz, vpx, wown, wbuf, nown,
    rc, c1, rq,
    s_rz, s_rx, s_sz, s_sx, s_rzx, s_rxz,
    v_rz, v_rx, v_sz, v_sx, v_rzx, v_rxz,
    load, send, recv, recv_w, recv_n,
):
    dp = lax.axis_index("dp")
    tensor = lax.axis_index("tensor")
    q, core = dp // NC, lax.rem(dp, NC)
    z, xh = tensor // NX, lax.rem(tensor, NX)
    xl, y = q // NY, lax.rem(q, NY)
    kv = v_out.shape[1]
    cols = v_sz.shape[2]

    def to_z(k):
        return lax.rem(z + k, NZ)

    def to_x(k):
        return lax.rem(xh + k, NX)

    def at_z(k):
        return (dp, to_z(k) * NX + xh)

    def at_x(k):
        return (dp, z * NX + to_x(k))

    def at_q(p):
        return (p * NC + core, tensor)

    def step_q(i):
        far = far_first(i // 2)
        side = lax.rem(xl + 1 - lax.rem(i, 2), 2) * NY
        return side + lax.rem(y + far, NY), side + lax.rem(y - far + NY, NY)

    other = (q * NC + (1 - core), tensor)
    barrier = pltpu.get_barrier_semaphore()

    def greet(device):
        pl.semaphore_signal(barrier, inc=1, device_id=device, device_id_type=MESH)

    loop(NQ - 1, lambda i: greet(at_q(step_q(i)[0])))
    loop(NZ - 1, lambda i: greet(at_z(far_first(i))))
    loop(NX - 1, lambda i: greet(at_x(i + 1)))
    greet(other)

    loads = [
        pltpu.make_async_copy(src, dst, load.at[i])
        for i, (src, dst) in enumerate((
            (xs_hbm, xs_ref), (dvs_hbm, dvs_ref), (m_hbm, m_ref),
            (xl_hbm, xl_ref), (dvl_hbm, dvl_ref),
            (m1_hbm, m1_ref), (m2_hbm, m2_ref),
        ))
    ]
    for copy in loads:
        copy.start()

    def remote(src, dst, slot, device, arrival=None):
        pltpu.make_async_remote_copy(
            src_ref=src, dst_ref=dst, send_sem=send.at[slot],
            recv_sem=recv.at[slot] if arrival is None else arrival,
            device_id=device, device_id_type=MESH,
        ).start()

    def wait(sem, ref):
        pltpu.make_async_copy(ref, ref, sem).wait()

    def to_other_chips(own, gathered, slot, arrivals):
        remote(own, gathered.at[q, core], slot + 1, other)
        loop(
            NQ - 1,
            lambda i: remote(
                own, gathered.at[q, core], slot, at_q(step_q(i)[0]), arrivals.at[i]
            ),
        )

    def on_to_other_core(gathered, slot, arrivals, between=None):
        def forward(i):
            chunk = gathered.at[step_q(i)[1], core]
            wait(arrivals.at[i], chunk)
            remote(chunk, chunk, slot + 1, other)

        loop(8, forward)
        if between is not None:
            loop(NQ - 1, between)
        loop(NQ - 9, lambda i: forward(i + 8))

    def first_stage(part_z, part_x, rz, rx, slot):
        def along_z(i):
            k = far_first(i)
            remote(part_z.at[to_z(k)], rz.at[k - 1], slot, at_z(k))

        loop(NZ - 1, along_z)
        for k in (2, 1, 3):
            remote(part_x.at[:, to_x(k)], rx.at[k - 1], slot + 1, at_x(k))

    def second_stage(part_z, part_x, rz, rx, sz, sx, rzx, rxz, slot):
        wait(recv.at[slot], rz)
        total = part_z[z].astype(F32)
        for k in range(NZ - 1):
            total += rz[k].astype(F32)
        sz[...] = total.astype(BF16)
        for k in (2, 1, 3):
            remote(sz.at[to_x(k)], rzx.at[k - 1], slot + 2, at_x(k))

        wait(recv.at[slot + 1], rx)
        total = part_x[:, xh].astype(F32)
        for k in range(NX - 1):
            total += rx[k].astype(F32)
        sx[...] = total.astype(BF16)

        def along_z(i):
            k = far_first(i)
            remote(sx.at[to_z(k)], rxz.at[k - 1], slot + 3, at_z(k))

        loop(NZ - 1, along_z)

    def last_sums(sz, sx, rzx, rxz, slot):
        wait(recv.at[slot + 2], rzx)
        left = sz[xh].astype(F32)
        for k in range(NX - 1):
            left += rzx[k].astype(F32)
        wait(recv.at[slot + 3], rxz)
        right = sx[z].astype(F32)
        for k in range(NZ - 1):
            right += rxz[k].astype(F32)
        return jnp.concatenate([left, right], axis=1)

    loads[0].wait()
    xsf[...] = xs_ref[...].astype(F32)
    rows = xs_ref.shape[0] // 2
    live = lax.broadcasted_iota(jnp.int32, (rows, xs_ref.shape[1]), 0) < slen_ref[0]
    x0 = jnp.where(live, xsf[pl.ds(0, rows, stride=2), :], 0.0).astype(BF16)
    x1 = jnp.where(live, xsf[pl.ds(1, rows, stride=2), :], 0.0).astype(BF16)
    loads[1].wait()
    dvs = dvs_ref[...]
    g0 = contract(x0, dvs, 0).reshape(16, 8, kv)
    g1 = contract(x1, dvs, 0).reshape(16, 8, kv)
    for s, owners in enumerate(swap_quads(g0, g1)):
        owners = owners.astype(BF16).reshape(NZ, 2, 8, kv)
        for p in range(2):
            gsz[:, 2 * p + s] = owners[:, p, :, :cols]
            gsx[:, 2 * p + s] = owners[:, p, :, cols:]

    loads[2].wait()
    w = jnp.concatenate([m_ref[0], m_ref[1]], axis=0).astype(BF16)
    wown[...] = w
    wbuf[q, core] = w

    loads[3].wait()
    quads = xl_ref[...].astype(F32).reshape(32, 2, 8, 128)
    blocks = swap_quads(quads[:, 0], quads[:, 1])
    x = jnp.concatenate([b.reshape(256, 128) for b in blocks], axis=1)
    live = lax.broadcasted_iota(jnp.int32, x.shape, 1) < llen_ref[0]
    x = jnp.where(live, x, 0.0).astype(BF16)
    xt[...] = x
    loads[4].wait()
    gl[...] = contract(x, dvl_ref[...], 1).astype(BF16).reshape(gl.shape)

    pl.semaphore_wait(barrier, NZ - 1 + NX - 1 + NQ - 1 + 1)
    remote(gl.at[:, 1 - core], rc, GC, other)
    to_other_chips(wown, wbuf, W, recv_w)
    first_stage(gsz, gsx, s_rz, s_rx, S1)

    wait(recv.at[GC], rc)

    def add(i):
        c1[i] = (gl[i, core].astype(F32) + rc[i].astype(F32)).astype(BF16)

    loop(NQ, add)

    def to_owner(i):
        to = step_q(i)[0]
        remote(c1.at[to], rq.at[i], GQ, at_q(to))


    on_to_other_core(wbuf, W, recv_w, to_owner)
    second_stage(gsz, gsx, s_rz, s_rx, s_sz, s_sx, s_rzx, s_rxz, S1)

    wait(recv.at[WF], wbuf.at[:, 1 - core])
    values = contract(xt[...], wbuf[...].reshape(NQ * NC * 8, kv), 0).astype(BF16)
    vpz[...] = values[:, :cols].reshape(vpz.shape)
    vpx[...] = values[:, cols:].reshape(vpx.shape)
    first_stage(vpz, vpx, v_rz, v_rx, V1)

    wait(recv.at[GQ], rq)
    grad = c1[q].astype(F32)
    for k in range(NQ - 1):
        grad += rq[k].astype(F32)
    grad += last_sums(s_sz, s_sx, s_rzx, s_rxz, S1)

    loads[5].wait()
    loads[6].wait()
    first_corr = 1.0 - 0.9**10
    second_corr = 1.0 - 0.999**10
    for a in range(2):
        ga = grad[4 * a : 4 * a + 4]
        master = m_ref[a]
        new1 = 0.9 * m1_ref[a] + 0.1 * ga
        new2 = 0.999 * m2_ref[a] + 0.001 * ga * ga
        update = new1 / first_corr / (jnp.sqrt(new2 / second_corr) + 1e-08)
        new_master = master - 0.01 * (update + 0.1 * master)
        nown[a] = new_master.astype(BF16)
        nm_out[a] = new_master
        nm1_out[a] = new1
        nm2_out[a] = new2
    to_other_chips(nown, nw_out, N, recv_n)
    nw_out[q, core] = nown[...]

    second_stage(vpz, vpx, v_rz, v_rx, v_sz, v_sx, v_rzx, v_rxz, V1)
    on_to_other_core(nw_out, N, recv_n)
    v_out[...] = last_sums(v_sz, v_sx, v_rzx, v_rxz, V1).astype(BF16)
    wait(recv.at[NF], nw_out.at[:, 1 - core])

    wait(send.at[W], rq)
    wait(send.at[WF], rc)
    wait(send.at[GC], rc)
    wait(send.at[GQ], rq)
    wait(send.at[N], rq)
    wait(send.at[NF], rc)
    for slot, (rz, rx, rzx, rxz) in (
        (S1, (s_rz, s_rx, s_rzx, s_rxz)),
        (V1, (v_rz, v_rx, v_rzx, v_rxz)),
    ):
        wait(send.at[slot], rz)
        wait(send.at[slot + 1], rx)
        wait(send.at[slot + 2], rzx)
        wait(send.at[slot + 3], rxz)


def hand_over(*refs):
    n = len(refs) // 2
    copies = [
        pltpu.make_async_copy(refs[i], refs[n + i], refs[-1].at[i]) for i in range(n)
    ]
    for copy in copies:
        copy.start()
    for copy in copies:
        copy.wait()


def body(x_long, dv_long, x_short, dv_short, long_len, short_len, master, moment1, moment2):
    kv = master.shape[2]
    cols = 5 * kv // 8
    rest = kv - cols
    rows_l, outer, inner = x_long.shape
    xl = jnp.transpose(x_long, (1, 2, 0)).reshape(outer, inner, rows_l // 128, 128)
    xl = jnp.transpose(xl, (0, 2, 1, 3)).reshape(-1, 128)
    xs = x_short.reshape(-1, x_short.shape[2])
    operands = (xl, dv_long, xs, dv_short, long_len, short_len, master, moment1, moment2)
    state = jax.ShapeDtypeStruct(master.shape, F32)
    outs = (
        jax.ShapeDtypeStruct((8, kv), BF16),
        state,
        state,
        state,
        jax.ShapeDtypeStruct((NQ, NC, 2, 4, kv), BF16),
    )
    vmem = pl.BlockSpec(memory_space=pltpu.VMEM)
    hbm = pl.BlockSpec(memory_space=pl.ANY)
    smem = pl.BlockSpec(memory_space=pltpu.SMEM)
    sums = [
        pltpu.VMEM((NZ - 1, NX, 8, cols), BF16),
        pltpu.VMEM((NX - 1, NZ, 8, rest), BF16),
        pltpu.VMEM((NX, 8, cols), BF16),
        pltpu.VMEM((NZ, 8, rest), BF16),
        pltpu.VMEM((NX - 1, 8, cols), BF16),
        pltpu.VMEM((NZ - 1, 8, rest), BF16),
    ]
    results = pl.pallas_call(
        kernel,
        out_shape=tuple(pltpu.VMEM(o.shape, o.dtype) for o in outs),
        in_specs=[hbm] * 4 + [smem] * 2 + [hbm] * 3,
        out_specs=(vmem,) * 5,
        scratch_shapes=[
            pltpu.VMEM(a.shape, a.dtype) for a in operands if a.dtype != jnp.int32
        ]
        + [
            pltpu.VMEM(xs.shape, F32),
            pltpu.VMEM((outer * inner, rows_l), BF16),
            pltpu.VMEM((NQ, NC, 8, kv), BF16),
            pltpu.VMEM((NZ, NX, 8, cols), BF16),
            pltpu.VMEM((NZ, NX, 8, rest), BF16),
            pltpu.VMEM((NZ, NX, 8, cols), BF16),
            pltpu.VMEM((NZ, NX, 8, rest), BF16),
            pltpu.VMEM((8, kv), BF16),
            pltpu.VMEM((NQ, NC, 8, kv), BF16),
            pltpu.VMEM((2, 4, kv), BF16),
            pltpu.VMEM((NQ, 8, kv), BF16),
            pltpu.VMEM((NQ, 8, kv), BF16),
            pltpu.VMEM((NQ - 1, 8, kv), BF16),
        ]
        + sums
        + sums
        + [
            pltpu.SemaphoreType.DMA((7,)),
            pltpu.SemaphoreType.DMA((14,)),
            pltpu.SemaphoreType.DMA((14,)),
            pltpu.SemaphoreType.DMA((NQ - 1,)),
            pltpu.SemaphoreType.DMA((NQ - 1,)),
        ],
        compiler_params=pltpu.CompilerParams(collective_id=0, has_side_effects=True),
    )(*operands)
    v, nm, nm1, nm2, nw = pl.pallas_call(
        hand_over,
        out_shape=outs,
        in_specs=[vmem] * 5,
        out_specs=(hbm,) * 5,
        scratch_shapes=[pltpu.SemaphoreType.DMA((5,))],
    )(*(pltpu.with_memory_space_constraint(r, pltpu.VMEM) for r in results))
    return v, nm, nm1, nm2, nw.reshape(NQ * NC * 2, 4, kv)


def solution(mesh):
    placed = (
        P("dp", None, "tensor"),
        P("dp", None),
        P("tensor", "dp", None),
        P("tensor", None),
        P("dp"),
        P("tensor"),
        P("dp", "tensor", None),
        P("dp", "tensor", None),
        P("dp", "tensor", None),
    )
    return jax.shard_map(
        body,
        mesh=mesh,
        in_specs=placed,
        out_specs=(
            P(("dp", "tensor"), None),
            P("dp", "tensor", None),
            P("dp", "tensor", None),
            P("dp", "tensor", None),
            P(None, "tensor", None),
        ),
        check_vma=False,
    )
```

```python
import jax
import jax.numpy as jnp
from jax import lax
from jax.experimental import pallas as pl
from jax.experimental.pallas import tpu as pltpu
from jax.sharding import PartitionSpec as P

MESH = pl.DeviceIdType.MESH
F32 = jnp.float32
BF16 = jnp.bfloat16

NZ, NX = 8, 4
NY, NC = 8, 2
NQ = 2 * NY
W, WF, GC, GQ, N, NF, S1, V1 = 0, 1, 2, 3, 4, 5, 6, 10


def contract(left, right, left_dim):
    return lax.dot_general(
        left, right, (((left_dim,), (0,)), ((), ())), preferred_element_type=F32
    )


def far_first(i):
    return (4 + (i + 1) // 2 * (2 * (i % 2) - 1)) % 8


def loop(n, f):
    for i in range(n):
        f(i)


def swap_quads(even, odd):
    low = lax.broadcasted_iota(jnp.int32, even.shape, 1) < 4
    return (
        jnp.where(low, even, pltpu.roll(odd, 4, 1)),
        jnp.where(low, pltpu.roll(even, 4, 1), odd),
    )


def kernel(
    xl_hbm, dvl_hbm, xs_hbm, dvs_hbm, llen_ref, slen_ref, m_hbm, m1_hbm, m2_hbm,
    v_out, nm_out, nm1_out, nm2_out, nw_out,
    xl_ref, dvl_ref, xs_ref, dvs_ref, m_ref, m1_ref, m2_ref,
    xsf, xt, gl, gsz, gsx, vpz, vpx, wown, wbuf, nown,
    rc, c1, rq,
    s_rz, s_rx, s_sz, s_sx, s_rzx, s_rxz,
    v_rz, v_rx, v_sz, v_sx, v_rzx, v_rxz,
    load, send, recv, recv_w, recv_n,
):
    dp = lax.axis_index("dp")
    tensor = lax.axis_index("tensor")
    q, core = dp // NC, lax.rem(dp, NC)
    z, xh = tensor // NX, lax.rem(tensor, NX)
    xl, y = q // NY, lax.rem(q, NY)
    kv = v_out.shape[1]
    cols = v_sz.shape[2]

    def to_z(k):
        return lax.rem(z + k, NZ)

    def to_x(k):
        return lax.rem(xh + k, NX)

    def at_z(k):
        return (dp, to_z(k) * NX + xh)

    def at_x(k):
        return (dp, z * NX + to_x(k))

    def at_q(p):
        return (p * NC + core, tensor)

    def step_q(i):
        far = far_first(i // 2)
        side = (xl if i % 2 else 1 - xl) * NY
        return side + lax.rem(y + far, NY), side + lax.rem(y - far + NY, NY)

    other = (q * NC + (1 - core), tensor)
    barrier = pltpu.get_barrier_semaphore()

    def greet(device):
        pl.semaphore_signal(barrier, inc=1, device_id=device, device_id_type=MESH)

    loop(NQ - 1, lambda i: greet(at_q(step_q(i)[0])))
    loop(NZ - 1, lambda i: greet(at_z(far_first(i))))
    loop(NX - 1, lambda i: greet(at_x(i + 1)))
    greet(other)

    loads = [
        pltpu.make_async_copy(src, dst, load.at[i])
        for i, (src, dst) in enumerate((
            (xs_hbm, xs_ref), (dvs_hbm, dvs_ref), (m_hbm, m_ref),
            (xl_hbm, xl_ref), (dvl_hbm, dvl_ref),
            (m1_hbm, m1_ref), (m2_hbm, m2_ref),
        ))
    ]
    for copy in loads:
        copy.start()

    def remote(src, dst, slot, device, arrival=None):
        pltpu.make_async_remote_copy(
            src_ref=src, dst_ref=dst, send_sem=send.at[slot],
            recv_sem=recv.at[slot] if arrival is None else arrival,
            device_id=device, device_id_type=MESH,
        ).start()

    def wait(sem, ref):
        pltpu.make_async_copy(ref, ref, sem).wait()

    def to_other_chips(own, gathered, slot, arrivals):
        remote(own, gathered.at[q, core], slot + 1, other)
        loop(
            NQ - 1,
            lambda i: remote(
                own, gathered.at[q, core], slot, at_q(step_q(i)[0]), arrivals.at[i]
            ),
        )

    def on_to_other_core(gathered, slot, arrivals, between=None):
        def forward(i):
            chunk = gathered.at[step_q(i)[1], core]
            wait(arrivals.at[i], chunk)
            remote(chunk, chunk, slot + 1, other)

        loop(8, forward)
        if between is not None:
            loop(NQ - 1, between)
        loop(NQ - 9, lambda i: forward(i + 8))

    def first_stage(part_z, part_x, rz, rx, slot):
        def along_z(i):
            k = far_first(i)
            remote(part_z.at[to_z(k)], rz.at[k - 1], slot, at_z(k))

        loop(NZ - 1, along_z)
        for k in (2, 1, 3):
            remote(part_x.at[:, to_x(k)], rx.at[k - 1], slot + 1, at_x(k))

    def second_stage(part_z, part_x, rz, rx, sz, sx, rzx, rxz, slot):
        wait(recv.at[slot], rz)
        total = part_z[z].astype(F32)
        for k in range(NZ - 1):
            total += rz[k].astype(F32)
        sz[...] = total.astype(BF16)
        for k in (2, 1, 3):
            remote(sz.at[to_x(k)], rzx.at[k - 1], slot + 2, at_x(k))

        wait(recv.at[slot + 1], rx)
        total = part_x[:, xh].astype(F32)
        for k in range(NX - 1):
            total += rx[k].astype(F32)
        sx[...] = total.astype(BF16)

        def along_z(i):
            k = far_first(i)
            remote(sx.at[to_z(k)], rxz.at[k - 1], slot + 3, at_z(k))

        loop(NZ - 1, along_z)

    def last_sums(sz, sx, rzx, rxz, slot):
        wait(recv.at[slot + 2], rzx)
        left = sz[xh].astype(F32)
        for k in range(NX - 1):
            left += rzx[k].astype(F32)
        wait(recv.at[slot + 3], rxz)
        right = sx[z].astype(F32)
        for k in range(NZ - 1):
            right += rxz[k].astype(F32)
        return jnp.concatenate([left, right], axis=1)

    loads[0].wait()
    xsf[...] = xs_ref[...].astype(F32)
    rows = xs_ref.shape[0] // 2
    live = lax.broadcasted_iota(jnp.int32, (rows, xs_ref.shape[1]), 0) < slen_ref[0]
    x0 = jnp.where(live, xsf[pl.ds(0, rows, stride=2), :], 0.0).astype(BF16)
    x1 = jnp.where(live, xsf[pl.ds(1, rows, stride=2), :], 0.0).astype(BF16)
    loads[1].wait()
    dvs = dvs_ref[...]
    g0 = contract(x0, dvs, 0).reshape(16, 8, kv)
    g1 = contract(x1, dvs, 0).reshape(16, 8, kv)
    for s, owners in enumerate(swap_quads(g0, g1)):
        owners = owners.astype(BF16).reshape(NZ, 2, 8, kv)
        for p in range(2):
            gsz[:, 2 * p + s] = owners[:, p, :, :cols]
            gsx[:, 2 * p + s] = owners[:, p, :, cols:]

    loads[2].wait()
    w = jnp.concatenate([m_ref[0], m_ref[1]], axis=0).astype(BF16)
    wown[...] = w
    wbuf[q, core] = w

    loads[3].wait()
    quads = xl_ref[...].astype(F32).reshape(32, 2, 8, 128)
    blocks = swap_quads(quads[:, 0], quads[:, 1])
    x = jnp.concatenate([b.reshape(256, 128) for b in blocks], axis=1)
    live = lax.broadcasted_iota(jnp.int32, x.shape, 1) < llen_ref[0]
    x = jnp.where(live, x, 0.0).astype(BF16)
    xt[...] = x
    loads[4].wait()
    gl[...] = contract(x, dvl_ref[...], 1).astype(BF16).reshape(gl.shape)

    pl.semaphore_wait(barrier, NZ - 1 + NX - 1 + NQ - 1 + 1)
    remote(gl.at[:, 1 - core], rc, GC, other)
    to_other_chips(wown, wbuf, W, recv_w)
    first_stage(gsz, gsx, s_rz, s_rx, S1)

    wait(recv.at[GC], rc)

    def add(i, c):
        c1[i] = (gl[i, core].astype(F32) + rc[i].astype(F32)).astype(BF16)
        return c

    lax.fori_loop(0, NQ, add, 0)

    def to_owner(i):
        to = step_q(i)[0]
        remote(c1.at[to], rq.at[i], GQ, at_q(to))


    on_to_other_core(wbuf, W, recv_w, to_owner)
    second_stage(gsz, gsx, s_rz, s_rx, s_sz, s_sx, s_rzx, s_rxz, S1)

    wait(recv.at[WF], wbuf.at[:, 1 - core])
    values = contract(xt[...], wbuf[...].reshape(NQ * NC * 8, kv), 0).astype(BF16)
    vpz[...] = values[:, :cols].reshape(vpz.shape)
    vpx[...] = values[:, cols:].reshape(vpx.shape)
    first_stage(vpz, vpx, v_rz, v_rx, V1)

    wait(recv.at[GQ], rq)
    grad = c1[q].astype(F32)
    for k in range(NQ - 1):
        grad += rq[k].astype(F32)
    grad += last_sums(s_sz, s_sx, s_rzx, s_rxz, S1)

    loads[5].wait()
    loads[6].wait()
    first_corr = 1.0 - 0.9**10
    second_corr = 1.0 - 0.999**10
    for a in range(2):
        ga = grad[4 * a : 4 * a + 4]
        master = m_ref[a]
        new1 = 0.9 * m1_ref[a] + 0.1 * ga
        new2 = 0.999 * m2_ref[a] + 0.001 * ga * ga
        update = new1 / first_corr / (jnp.sqrt(new2 / second_corr) + 1e-08)
        new_master = master - 0.01 * (update + 0.1 * master)
        nown[a] = new_master.astype(BF16)
        nm_out[a] = new_master
        nm1_out[a] = new1
        nm2_out[a] = new2
    to_other_chips(nown, nw_out, N, recv_n)
    nw_out[q, core] = nown[...]

    second_stage(vpz, vpx, v_rz, v_rx, v_sz, v_sx, v_rzx, v_rxz, V1)
    on_to_other_core(nw_out, N, recv_n)
    v_out[...] = last_sums(v_sz, v_sx, v_rzx, v_rxz, V1).astype(BF16)
    wait(recv.at[NF], nw_out.at[:, 1 - core])

    wait(send.at[W], rq)
    wait(send.at[WF], rc)
    wait(send.at[GC], rc)
    wait(send.at[GQ], rq)
    wait(send.at[N], rq)
    wait(send.at[NF], rc)
    for slot, (rz, rx, rzx, rxz) in (
        (S1, (s_rz, s_rx, s_rzx, s_rxz)),
        (V1, (v_rz, v_rx, v_rzx, v_rxz)),
    ):
        wait(send.at[slot], rz)
        wait(send.at[slot + 1], rx)
        wait(send.at[slot + 2], rzx)
        wait(send.at[slot + 3], rxz)


def hand_over(*refs):
    n = len(refs) // 2
    copies = [
        pltpu.make_async_copy(refs[i], refs[n + i], refs[-1].at[i]) for i in range(n)
    ]
    for copy in copies:
        copy.start()
    for copy in copies:
        copy.wait()


def body(x_long, dv_long, x_short, dv_short, long_len, short_len, master, moment1, moment2):
    kv = master.shape[2]
    cols = 5 * kv // 8
    rest = kv - cols
    rows_l, outer, inner = x_long.shape
    xl = jnp.transpose(x_long, (1, 2, 0)).reshape(outer, inner, rows_l // 128, 128)
    xl = jnp.transpose(xl, (0, 2, 1, 3)).reshape(-1, 128)
    xs = x_short.reshape(-1, x_short.shape[2])
    operands = (xl, dv_long, xs, dv_short, long_len, short_len, master, moment1, moment2)
    state = jax.ShapeDtypeStruct(master.shape, F32)
    outs = (
        jax.ShapeDtypeStruct((8, kv), BF16),
        state,
        state,
        state,
        jax.ShapeDtypeStruct((NQ, NC, 2, 4, kv), BF16),
    )
    vmem = pl.BlockSpec(memory_space=pltpu.VMEM)
    hbm = pl.BlockSpec(memory_space=pl.ANY)
    smem = pl.BlockSpec(memory_space=pltpu.SMEM)
    sums = [
        pltpu.VMEM((NZ - 1, NX, 8, cols), BF16),
        pltpu.VMEM((NX - 1, NZ, 8, rest), BF16),
        pltpu.VMEM((NX, 8, cols), BF16),
        pltpu.VMEM((NZ, 8, rest), BF16),
        pltpu.VMEM((NX - 1, 8, cols), BF16),
        pltpu.VMEM((NZ - 1, 8, rest), BF16),
    ]
    results = pl.pallas_call(
        kernel,
        out_shape=tuple(pltpu.VMEM(o.shape, o.dtype) for o in outs),
        in_specs=[hbm] * 4 + [smem] * 2 + [hbm] * 3,
        out_specs=(vmem,) * 5,
        scratch_shapes=[
            pltpu.VMEM(a.shape, a.dtype) for a in operands if a.dtype != jnp.int32
        ]
        + [
            pltpu.VMEM(xs.shape, F32),
            pltpu.VMEM((outer * inner, rows_l), BF16),
            pltpu.VMEM((NQ, NC, 8, kv), BF16),
            pltpu.VMEM((NZ, NX, 8, cols), BF16),
            pltpu.VMEM((NZ, NX, 8, rest), BF16),
            pltpu.VMEM((NZ, NX, 8, cols), BF16),
            pltpu.VMEM((NZ, NX, 8, rest), BF16),
            pltpu.VMEM((8, kv), BF16),
            pltpu.VMEM((NQ, NC, 8, kv), BF16),
            pltpu.VMEM((2, 4, kv), BF16),
            pltpu.VMEM((NQ, 8, kv), BF16),
            pltpu.VMEM((NQ, 8, kv), BF16),
            pltpu.VMEM((NQ - 1, 8, kv), BF16),
        ]
        + sums
        + sums
        + [
            pltpu.SemaphoreType.DMA((7,)),
            pltpu.SemaphoreType.DMA((14,)),
            pltpu.SemaphoreType.DMA((14,)),
            pltpu.SemaphoreType.DMA((NQ - 1,)),
            pltpu.SemaphoreType.DMA((NQ - 1,)),
        ],
        compiler_params=pltpu.CompilerParams(collective_id=0, has_side_effects=True),
    )(*operands)
    v, nm, nm1, nm2, nw = pl.pallas_call(
        hand_over,
        out_shape=outs,
        in_specs=[vmem] * 5,
        out_specs=(hbm,) * 5,
        scratch_shapes=[pltpu.SemaphoreType.DMA((5,))],
    )(*(pltpu.with_memory_space_constraint(r, pltpu.VMEM) for r in results))
    return v, nm, nm1, nm2, nw.reshape(NQ * NC * 2, 4, kv)


def solution(mesh):
    placed = (
        P("dp", None, "tensor"),
        P("dp", None),
        P("tensor", "dp", None),
        P("tensor", None),
        P("dp"),
        P("tensor"),
        P("dp", "tensor", None),
        P("dp", "tensor", None),
        P("dp", "tensor", None),
    )
    return jax.shard_map(
        body,
        mesh=mesh,
        in_specs=placed,
        out_specs=(
            P(("dp", "tensor"), None),
            P("dp", "tensor", None),
            P("dp", "tensor", None),
            P("dp", "tensor", None),
            P(None, "tensor", None),
        ),
        check_vma=False,
    )
```

```python
import jax
import jax.numpy as jnp
from jax import lax
from jax.experimental import pallas as pl
from jax.experimental.pallas import tpu as pltpu
from jax.sharding import PartitionSpec as P

MESH = pl.DeviceIdType.MESH
F32 = jnp.float32
BF16 = jnp.bfloat16

NZ, NX = 8, 4
NY, NC = 8, 2
NQ = 2 * NY
W, WF, N, NF, GC, GQ, S1, V1 = 0, 2, 4, 6, 8, 9, 10, 14


def contract(left, right, left_dim):
    return lax.dot_general(
        left, right, (((left_dim,), (0,)), ((), ())), preferred_element_type=F32
    )


def far_first(i):
    return (4 + (i + 1) // 2 * (2 * (i % 2) - 1)) % 8


def loop(n, f):
    for i in range(n):
        f(i)


def swap_quads(even, odd):
    low = lax.broadcasted_iota(jnp.int32, even.shape, 1) < 4
    return (
        jnp.where(low, even, pltpu.roll(odd, 4, 1)),
        jnp.where(low, pltpu.roll(even, 4, 1), odd),
    )


def kernel(
    xl_hbm, dvl_hbm, xs_hbm, dvs_hbm, llen_ref, slen_ref, m_hbm, m1_hbm, m2_hbm,
    v_out, nm_out, nm1_out, nm2_out, nw_out,
    xl_ref, dvl_ref, xs_ref, dvs_ref, m_ref, m1_ref, m2_ref,
    xsf, xt, gl, gsz, gsx, vpz, vpx, wown, wbuf, nown,
    rc, c1, rq,
    s_rz, s_rx, s_sz, s_sx, s_rzx, s_rxz,
    v_rz, v_rx, v_sz, v_sx, v_rzx, v_rxz,
    load, send, recv, recv_w, recv_n,
):
    dp = lax.axis_index("dp")
    tensor = lax.axis_index("tensor")
    q, core = dp // NC, lax.rem(dp, NC)
    z, xh = tensor // NX, lax.rem(tensor, NX)
    xl, y = q // NY, lax.rem(q, NY)
    kv = v_out.shape[1]
    cols = v_sz.shape[2]

    def to_z(k):
        return lax.rem(z + k, NZ)

    def to_x(k):
        return lax.rem(xh + k, NX)

    def at_z(k):
        return (dp, to_z(k) * NX + xh)

    def at_x(k):
        return (dp, z * NX + to_x(k))

    def at_q(p):
        return (p * NC + core, tensor)

    def step_q(i):
        far = far_first(i // 2)
        side = (xl if i % 2 else 1 - xl) * NY
        return side + lax.rem(y + far, NY), side + lax.rem(y - far + NY, NY)

    other = (q * NC + (1 - core), tensor)
    barrier = pltpu.get_barrier_semaphore()

    def greet(device):
        pl.semaphore_signal(barrier, inc=1, device_id=device, device_id_type=MESH)

    loop(NQ - 1, lambda i: greet(at_q(step_q(i)[0])))
    loop(NZ - 1, lambda i: greet(at_z(far_first(i))))
    loop(NX - 1, lambda i: greet(at_x(i + 1)))
    greet(other)

    loads = [
        pltpu.make_async_copy(src, dst, load.at[i])
        for i, (src, dst) in enumerate((
            (xs_hbm, xs_ref), (dvs_hbm, dvs_ref), (m_hbm, m_ref),
            (xl_hbm, xl_ref), (dvl_hbm, dvl_ref),
            (m1_hbm, m1_ref), (m2_hbm, m2_ref),
        ))
    ]
    for copy in loads:
        copy.start()

    def remote(src, dst, slot, device, arrival=None):
        pltpu.make_async_remote_copy(
            src_ref=src, dst_ref=dst, send_sem=send.at[slot],
            recv_sem=recv.at[slot] if arrival is None else arrival,
            device_id=device, device_id_type=MESH,
        ).start()

    def wait(sem, ref):
        pltpu.make_async_copy(ref, ref, sem).wait()

    parts = (slice(0, cols), slice(cols, kv))

    def to_other_chips(p, own, gathered, slot, arrivals):
        mine = own.at[..., parts[p]]
        there = gathered.at[q, core].at[..., parts[p]]
        remote(mine, there, slot + 2 + p, other)
        loop(
            NQ - 1,
            lambda i: remote(
                mine, there, slot + p, at_q(step_q(i)[0]), arrivals.at[p, i // 2]
            ),
        )

    def on_to_other_core(p, gathered, slot, arrivals):
        for pair in range(NY):
            steps = range(2 * pair, min(2 * pair + 2, NQ - 1))
            arrived = gathered.at[pl.ds(0, len(steps)), core]
            wait(arrivals.at[p, pair], arrived.at[..., parts[p]])
            for i in steps:
                chunk = gathered.at[step_q(i)[1], core].at[..., parts[p]]
                remote(chunk, chunk, slot + 2 + p, other)

    def of_other_core(p, gathered, slot):
        wait(recv.at[slot + 2 + p], gathered.at[:, 1 - core].at[..., parts[p]])

    def all_sent(gathered, slot):
        for p in range(2):
            sent = gathered.at[pl.ds(0, NQ - 1), core]
            wait(send.at[slot + p], sent.at[..., parts[p]])
            wait(send.at[slot + 2 + p], gathered.at[:, core].at[..., parts[p]])

    def first_z(part, rz, slot):
        for i in range(NZ - 1):
            k = far_first(i)
            remote(part.at[to_z(k)], rz.at[k - 1], slot, at_z(k))

    def first_x(part, rx, slot):
        for k in (2, 1, 3):
            remote(part.at[:, to_x(k)], rx.at[k - 1], slot + 1, at_x(k))

    def second_z(part, rz, sz, rzx, slot):
        wait(recv.at[slot], rz)
        total = part[z].astype(F32)
        for k in range(NZ - 1):
            total += rz[k].astype(F32)
        sz[...] = total.astype(BF16)
        for k in (2, 1, 3):
            remote(sz.at[to_x(k)], rzx.at[k - 1], slot + 2, at_x(k))

    def second_x(part, rx, sx, rxz, slot):
        wait(recv.at[slot + 1], rx)
        total = part[:, xh].astype(F32)
        for k in range(NX - 1):
            total += rx[k].astype(F32)
        sx[...] = total.astype(BF16)
        for i in range(NZ - 1):
            k = far_first(i)
            remote(sx.at[to_z(k)], rxz.at[k - 1], slot + 3, at_z(k))

    def last_z(sz, rzx, slot):
        wait(recv.at[slot + 2], rzx)
        total = sz[xh].astype(F32)
        for k in range(NX - 1):
            total += rzx[k].astype(F32)
        return total

    def last_x(sx, rxz, slot):
        wait(recv.at[slot + 3], rxz)
        total = sx[z].astype(F32)
        for k in range(NZ - 1):
            total += rxz[k].astype(F32)
        return total

    loads[0].wait()
    xsf[...] = xs_ref[...].astype(F32)
    rows = xs_ref.shape[0] // 2
    live = lax.broadcasted_iota(jnp.int32, (rows, xs_ref.shape[1]), 0) < slen_ref[0]
    x0 = jnp.where(live, xsf[pl.ds(0, rows, stride=2), :], 0.0).astype(BF16)
    x1 = jnp.where(live, xsf[pl.ds(1, rows, stride=2), :], 0.0).astype(BF16)
    loads[1].wait()
    dvs = dvs_ref[...]
    g0 = contract(x0, dvs, 0).reshape(16, 8, kv)
    g1 = contract(x1, dvs, 0).reshape(16, 8, kv)
    for s, owners in enumerate(swap_quads(g0, g1)):
        owners = owners.astype(BF16).reshape(NZ, 2, 8, kv)
        for p in range(2):
            gsz[:, 2 * p + s] = owners[:, p, :, :cols]
            gsx[:, 2 * p + s] = owners[:, p, :, cols:]

    loads[2].wait()
    w = jnp.concatenate([m_ref[0], m_ref[1]], axis=0).astype(BF16)
    wown[...] = w
    wbuf[q, core] = w

    loads[3].wait()
    quads = xl_ref[...].astype(F32).reshape(32, 2, 8, 128)
    blocks = swap_quads(quads[:, 0], quads[:, 1])
    x = jnp.concatenate([b.reshape(256, 128) for b in blocks], axis=1)
    live = lax.broadcasted_iota(jnp.int32, x.shape, 1) < llen_ref[0]
    x = jnp.where(live, x, 0.0).astype(BF16)
    xt[...] = x
    loads[4].wait()
    gl[...] = contract(x, dvl_ref[...], 1).astype(BF16).reshape(gl.shape)

    pl.semaphore_wait(barrier, NZ - 1 + NX - 1 + NQ - 1 + 1)
    remote(gl.at[:, 1 - core], rc, GC, other)
    to_other_chips(0, wown, wbuf, W, recv_w)
    first_z(gsz, s_rz, S1)
    first_x(gsx, s_rx, S1)
    to_other_chips(1, wown, wbuf, W, recv_w)

    wait(recv.at[GC], rc)

    def add(i, c):
        c1[i] = (gl[i, core].astype(F32) + rc[i].astype(F32)).astype(BF16)
        return c

    lax.fori_loop(0, NQ, add, 0)

    on_to_other_core(0, wbuf, W, recv_w)
    for i in range(NQ - 1):
        to = step_q(i)[0]
        remote(c1.at[to], rq.at[i], GQ, at_q(to))

    second_x(gsx, s_rx, s_sx, s_rxz, S1)
    of_other_core(0, wbuf, W)
    weights = wbuf[:, :, :, :cols].reshape(NQ * NC * 8, cols)
    vpz[...] = contract(xt[...], weights, 0).astype(BF16).reshape(vpz.shape)
    first_z(vpz, v_rz, V1)

    on_to_other_core(1, wbuf, W, recv_w)
    second_z(gsz, s_rz, s_sz, s_rzx, S1)
    of_other_core(1, wbuf, W)
    weights = wbuf[:, :, :, cols:].reshape(NQ * NC * 8, kv - cols)
    vpx[...] = contract(xt[...], weights, 0).astype(BF16).reshape(vpx.shape)
    first_x(vpx, v_rx, V1)

    loads[5].wait()
    loads[6].wait()
    wait(recv.at[GQ], rq)
    first_corr = 1.0 - 0.9**10
    second_corr = 1.0 - 0.999**10

    def update(p, short):
        part = parts[p]
        grad = short + c1[q, :, part].astype(F32)
        for k in range(NQ - 1):
            grad += rq[k, :, part].astype(F32)
        for a in range(2):
            ga = grad[4 * a : 4 * a + 4]
            master = m_ref[a, :, part]
            new1 = 0.9 * m1_ref[a, :, part] + 0.1 * ga
            new2 = 0.999 * m2_ref[a, :, part] + 0.001 * ga * ga
            step = new1 / first_corr / (jnp.sqrt(new2 / second_corr) + 1e-08)
            new_master = master - 0.01 * (step + 0.1 * master)
            nown[a, :, part] = new_master.astype(BF16)
            nm_out[a, :, part] = new_master
            nm1_out[a, :, part] = new1
            nm2_out[a, :, part] = new2
            nw_out[q, core, a, :, part] = new_master.astype(BF16)
        to_other_chips(p, nown, nw_out, N, recv_n)

    update(1, last_x(s_sx, s_rxz, S1))
    update(0, last_z(s_sz, s_rzx, S1))

    second_x(vpx, v_rx, v_sx, v_rxz, V1)
    second_z(vpz, v_rz, v_sz, v_rzx, V1)
    on_to_other_core(1, nw_out, N, recv_n)
    on_to_other_core(0, nw_out, N, recv_n)
    v_out[:, cols:] = last_x(v_sx, v_rxz, V1).astype(BF16)
    v_out[:, :cols] = last_z(v_sz, v_rzx, V1).astype(BF16)
    of_other_core(1, nw_out, N)
    of_other_core(0, nw_out, N)

    all_sent(wbuf, W)
    all_sent(nw_out, N)
    wait(send.at[GC], rc)
    wait(send.at[GQ], rq)
    for slot, (rz, rx, rzx, rxz) in (
        (S1, (s_rz, s_rx, s_rzx, s_rxz)),
        (V1, (v_rz, v_rx, v_rzx, v_rxz)),
    ):
        wait(send.at[slot], rz)
        wait(send.at[slot + 1], rx)
        wait(send.at[slot + 2], rzx)
        wait(send.at[slot + 3], rxz)


def hand_over(*refs):
    n = len(refs) // 2
    copies = [
        pltpu.make_async_copy(refs[i], refs[n + i], refs[-1].at[i]) for i in range(n)
    ]
    for copy in copies:
        copy.start()
    for copy in copies:
        copy.wait()


def body(x_long, dv_long, x_short, dv_short, long_len, short_len, master, moment1, moment2):
    kv = master.shape[2]
    cols = 5 * kv // 8
    rest = kv - cols
    rows_l, outer, inner = x_long.shape
    xl = jnp.transpose(x_long, (1, 2, 0)).reshape(outer, inner, rows_l // 128, 128)
    xl = jnp.transpose(xl, (0, 2, 1, 3)).reshape(-1, 128)
    xs = x_short.reshape(-1, x_short.shape[2])
    operands = (xl, dv_long, xs, dv_short, long_len, short_len, master, moment1, moment2)
    state = jax.ShapeDtypeStruct(master.shape, F32)
    outs = (
        jax.ShapeDtypeStruct((8, kv), BF16),
        state,
        state,
        state,
        jax.ShapeDtypeStruct((NQ, NC, 2, 4, kv), BF16),
    )
    vmem = pl.BlockSpec(memory_space=pltpu.VMEM)
    hbm = pl.BlockSpec(memory_space=pl.ANY)
    smem = pl.BlockSpec(memory_space=pltpu.SMEM)
    sums = [
        pltpu.VMEM((NZ - 1, NX, 8, cols), BF16),
        pltpu.VMEM((NX - 1, NZ, 8, rest), BF16),
        pltpu.VMEM((NX, 8, cols), BF16),
        pltpu.VMEM((NZ, 8, rest), BF16),
        pltpu.VMEM((NX - 1, 8, cols), BF16),
        pltpu.VMEM((NZ - 1, 8, rest), BF16),
    ]
    results = pl.pallas_call(
        kernel,
        out_shape=tuple(pltpu.VMEM(o.shape, o.dtype) for o in outs),
        in_specs=[hbm] * 4 + [smem] * 2 + [hbm] * 3,
        out_specs=(vmem,) * 5,
        scratch_shapes=[
            pltpu.VMEM(a.shape, a.dtype) for a in operands if a.dtype != jnp.int32
        ]
        + [
            pltpu.VMEM(xs.shape, F32),
            pltpu.VMEM((outer * inner, rows_l), BF16),
            pltpu.VMEM((NQ, NC, 8, kv), BF16),
            pltpu.VMEM((NZ, NX, 8, cols), BF16),
            pltpu.VMEM((NZ, NX, 8, rest), BF16),
            pltpu.VMEM((NZ, NX, 8, cols), BF16),
            pltpu.VMEM((NZ, NX, 8, rest), BF16),
            pltpu.VMEM((8, kv), BF16),
            pltpu.VMEM((NQ, NC, 8, kv), BF16),
            pltpu.VMEM((2, 4, kv), BF16),
            pltpu.VMEM((NQ, 8, kv), BF16),
            pltpu.VMEM((NQ, 8, kv), BF16),
            pltpu.VMEM((NQ - 1, 8, kv), BF16),
        ]
        + sums
        + sums
        + [
            pltpu.SemaphoreType.DMA((7,)),
            pltpu.SemaphoreType.DMA((18,)),
            pltpu.SemaphoreType.DMA((18,)),
            pltpu.SemaphoreType.DMA((2, NY)),
            pltpu.SemaphoreType.DMA((2, NY)),
        ],
        compiler_params=pltpu.CompilerParams(collective_id=0, has_side_effects=True),
    )(*operands)
    v, nm, nm1, nm2, nw = pl.pallas_call(
        hand_over,
        out_shape=outs,
        in_specs=[vmem] * 5,
        out_specs=(hbm,) * 5,
        scratch_shapes=[pltpu.SemaphoreType.DMA((5,))],
    )(*(pltpu.with_memory_space_constraint(r, pltpu.VMEM) for r in results))
    return v, nm, nm1, nm2, nw.reshape(NQ * NC * 2, 4, kv)


def solution(mesh):
    placed = (
        P("dp", None, "tensor"),
        P("dp", None),
        P("tensor", "dp", None),
        P("tensor", None),
        P("dp"),
        P("tensor"),
        P("dp", "tensor", None),
        P("dp", "tensor", None),
        P("dp", "tensor", None),
    )
    return jax.shard_map(
        body,
        mesh=mesh,
        in_specs=placed,
        out_specs=(
            P(("dp", "tensor"), None),
            P("dp", "tensor", None),
            P("dp", "tensor", None),
            P("dp", "tensor", None),
            P(None, "tensor", None),
        ),
        check_vma=False,
    )
```

```python
import jax
import jax.numpy as jnp
from jax import lax
from jax.experimental import pallas as pl
from jax.experimental.pallas import tpu as pltpu
from jax.sharding import PartitionSpec as P

MESH = pl.DeviceIdType.MESH
F32 = jnp.float32
BF16 = jnp.bfloat16

NZ, NX = 8, 4
NY, NC = 8, 2
NQ = 2 * NY
W, WF, N, NF, GC, GQ, S1, V1 = 0, 2, 4, 6, 8, 9, 10, 14


def contract(left, right, left_dim):
    return lax.dot_general(
        left, right, (((left_dim,), (0,)), ((), ())), preferred_element_type=F32
    )


def far_first(i):
    return (4 + (i + 1) // 2 * (2 * (i % 2) - 1)) % 8


def loop(n, f):
    for i in range(n):
        f(i)


def swap_quads(even, odd):
    low = lax.broadcasted_iota(jnp.int32, even.shape, 1) < 4
    return (
        jnp.where(low, even, pltpu.roll(odd, 4, 1)),
        jnp.where(low, pltpu.roll(even, 4, 1), odd),
    )


def kernel(
    xl_hbm, dvl_hbm, xs_hbm, dvs_hbm, llen_ref, slen_ref, m_hbm, m1_hbm, m2_hbm,
    v_out, nm_out, nm1_out, nm2_out, nw_out,
    xl_ref, dvl_ref, xs_ref, dvs_ref, m_ref, m1_ref, m2_ref,
    xsf, xt, gl, gsz, gsx, vpz, vpx, wown, wbuf, nown,
    rc, c1, rq,
    s_rz, s_rx, s_sz, s_sx, s_rzx, s_rxz,
    v_rz, v_rx, v_sz, v_sx, v_rzx, v_rxz,
    load, send, recv, recv_w, recv_n,
):
    dp = lax.axis_index("dp")
    tensor = lax.axis_index("tensor")
    q, core = dp // NC, lax.rem(dp, NC)
    z, xh = tensor // NX, lax.rem(tensor, NX)
    xl, y = q // NY, lax.rem(q, NY)
    kv = v_out.shape[1]
    cols = v_sz.shape[2]

    def to_z(k):
        return lax.rem(z + k, NZ)

    def to_x(k):
        return lax.rem(xh + k, NX)

    def at_z(k):
        return (dp, to_z(k) * NX + xh)

    def at_x(k):
        return (dp, z * NX + to_x(k))

    def at_q(p):
        return (p * NC + core, tensor)

    def step_q(i):
        far = far_first(i // 2)
        side = (xl if i % 2 else 1 - xl) * NY
        return side + lax.rem(y + far, NY), side + lax.rem(y - far + NY, NY)

    other = (q * NC + (1 - core), tensor)
    barrier = pltpu.get_barrier_semaphore()

    def greet(device):
        pl.semaphore_signal(barrier, inc=1, device_id=device, device_id_type=MESH)

    loop(NQ - 1, lambda i: greet(at_q(step_q(i)[0])))
    loop(NZ - 1, lambda i: greet(at_z(far_first(i))))
    loop(NX - 1, lambda i: greet(at_x(i + 1)))
    greet(other)

    loads = [
        pltpu.make_async_copy(src, dst, load.at[i])
        for i, (src, dst) in enumerate((
            (xs_hbm, xs_ref), (dvs_hbm, dvs_ref), (m_hbm, m_ref),
            (xl_hbm, xl_ref), (dvl_hbm, dvl_ref),
            (m1_hbm, m1_ref), (m2_hbm, m2_ref),
        ))
    ]
    for copy in loads:
        copy.start()

    def remote(src, dst, slot, device, arrival=None):
        pltpu.make_async_remote_copy(
            src_ref=src, dst_ref=dst, send_sem=send.at[slot],
            recv_sem=recv.at[slot] if arrival is None else arrival,
            device_id=device, device_id_type=MESH,
        ).start()

    def wait(sem, ref):
        pltpu.make_async_copy(ref, ref, sem).wait()

    parts = (slice(0, cols), slice(cols, kv))

    def to_other_chips(p, own, gathered, slot, arrivals):
        mine = own.at[..., parts[p]]
        there = gathered.at[q, core].at[..., parts[p]]
        remote(mine, there, slot + 2 + p, other)
        loop(
            NQ - 1,
            lambda i: remote(
                mine, there, slot + p, at_q(step_q(i)[0]), arrivals.at[p, i // 2]
            ),
        )

    def on_to_other_core(p, gathered, slot, arrivals):
        for pair in range(NY):
            steps = range(2 * pair, min(2 * pair + 2, NQ - 1))
            arrived = gathered.at[pl.ds(0, len(steps)), core]
            wait(arrivals.at[p, pair], arrived.at[..., parts[p]])
            for i in steps:
                chunk = gathered.at[step_q(i)[1], core].at[..., parts[p]]
                remote(chunk, chunk, slot + 2 + p, other)

    def of_other_core(p, gathered, slot):
        wait(recv.at[slot + 2 + p], gathered.at[:, 1 - core].at[..., parts[p]])

    def all_sent(gathered, slot):
        for p in range(2):
            sent = gathered.at[pl.ds(0, NQ - 1), core]
            wait(send.at[slot + p], sent.at[..., parts[p]])
            wait(send.at[slot + 2 + p], gathered.at[:, core].at[..., parts[p]])

    def first_z(part, rz, slot):
        for i in range(NZ - 1):
            k = far_first(i)
            remote(part.at[to_z(k)], rz.at[k - 1], slot, at_z(k))

    def first_x(part, rx, slot):
        for k in (2, 1, 3):
            remote(part.at[:, to_x(k)], rx.at[k - 1], slot + 1, at_x(k))

    def second_z(part, rz, sz, rzx, slot):
        wait(recv.at[slot], rz)
        total = part[z].astype(F32)
        for k in range(NZ - 1):
            total += rz[k].astype(F32)
        sz[...] = total.astype(BF16)
        for k in (2, 1, 3):
            remote(sz.at[to_x(k)], rzx.at[k - 1], slot + 2, at_x(k))

    def second_x(part, rx, sx, rxz, slot):
        wait(recv.at[slot + 1], rx)
        total = part[:, xh].astype(F32)
        for k in range(NX - 1):
            total += rx[k].astype(F32)
        sx[...] = total.astype(BF16)
        for i in range(NZ - 1):
            k = far_first(i)
            remote(sx.at[to_z(k)], rxz.at[k - 1], slot + 3, at_z(k))

    def last_z(sz, rzx, slot):
        wait(recv.at[slot + 2], rzx)
        total = sz[xh].astype(F32)
        for k in range(NX - 1):
            total += rzx[k].astype(F32)
        return total

    def last_x(sx, rxz, slot):
        wait(recv.at[slot + 3], rxz)
        total = sx[z].astype(F32)
        for k in range(NZ - 1):
            total += rxz[k].astype(F32)
        return total

    loads[0].wait()
    xsf[...] = xs_ref[...].astype(F32)
    rows = xs_ref.shape[0] // 2
    live = lax.broadcasted_iota(jnp.int32, (rows, xs_ref.shape[1]), 0) < slen_ref[0]
    x0 = jnp.where(live, xsf[pl.ds(0, rows, stride=2), :], 0.0).astype(BF16)
    x1 = jnp.where(live, xsf[pl.ds(1, rows, stride=2), :], 0.0).astype(BF16)
    loads[1].wait()
    dvs = dvs_ref[...]
    g0 = contract(x0, dvs, 0).reshape(16, 8, kv)
    g1 = contract(x1, dvs, 0).reshape(16, 8, kv)
    for s, owners in enumerate(swap_quads(g0, g1)):
        owners = owners.astype(BF16).reshape(NZ, 2, 8, kv)
        for p in range(2):
            gsz[:, 2 * p + s] = owners[:, p, :, :cols]
            gsx[:, 2 * p + s] = owners[:, p, :, cols:]

    loads[2].wait()
    w = jnp.concatenate([m_ref[0], m_ref[1]], axis=0).astype(BF16)
    wown[...] = w
    wbuf[q, core] = w

    loads[3].wait()
    quads = xl_ref[...].astype(F32).reshape(32, 2, 8, 128)
    blocks = swap_quads(quads[:, 0], quads[:, 1])
    x = jnp.concatenate([b.reshape(256, 128) for b in blocks], axis=1)
    live = lax.broadcasted_iota(jnp.int32, x.shape, 1) < llen_ref[0]
    x = jnp.where(live, x, 0.0).astype(BF16)
    xt[...] = x
    loads[4].wait()
    gl[...] = contract(x, dvl_ref[...], 1).astype(BF16).reshape(gl.shape)

    pl.semaphore_wait(barrier, NZ - 1 + NX - 1 + NQ - 1 + 1)
    remote(gl.at[:, 1 - core], rc, GC, other)
    to_other_chips(0, wown, wbuf, W, recv_w)
    first_z(gsz, s_rz, S1)
    first_x(gsx, s_rx, S1)
    to_other_chips(1, wown, wbuf, W, recv_w)

    wait(recv.at[GC], rc)

    def add(i, c):
        c1[i] = (gl[i, core].astype(F32) + rc[i].astype(F32)).astype(BF16)
        return c

    lax.fori_loop(0, NQ, add, 0)

    for i in range(NQ - 1):
        to = step_q(i)[0]
        remote(c1.at[to], rq.at[i], GQ, at_q(to))

    on_to_other_core(0, wbuf, W, recv_w)

    second_x(gsx, s_rx, s_sx, s_rxz, S1)
    of_other_core(0, wbuf, W)
    weights = wbuf[:, :, :, :cols].reshape(NQ * NC * 8, cols)
    vpz[...] = contract(xt[...], weights, 0).astype(BF16).reshape(vpz.shape)
    first_z(vpz, v_rz, V1)

    second_z(gsz, s_rz, s_sz, s_rzx, S1)
    on_to_other_core(1, wbuf, W, recv_w)
    of_other_core(1, wbuf, W)
    weights = wbuf[:, :, :, cols:].reshape(NQ * NC * 8, kv - cols)
    vpx[...] = contract(xt[...], weights, 0).astype(BF16).reshape(vpx.shape)
    first_x(vpx, v_rx, V1)

    loads[5].wait()
    loads[6].wait()
    wait(recv.at[GQ], rq)
    first_corr = 1.0 - 0.9**10
    second_corr = 1.0 - 0.999**10

    def update(p, short):
        part = parts[p]
        grad = short + c1[q, :, part].astype(F32)
        for k in range(NQ - 1):
            grad += rq[k, :, part].astype(F32)
        for a in range(2):
            ga = grad[4 * a : 4 * a + 4]
            master = m_ref[a, :, part]
            new1 = 0.9 * m1_ref[a, :, part] + 0.1 * ga
            new2 = 0.999 * m2_ref[a, :, part] + 0.001 * ga * ga
            step = new1 / first_corr / (jnp.sqrt(new2 / second_corr) + 1e-08)
            new_master = master - 0.01 * (step + 0.1 * master)
            nown[a, :, part] = new_master.astype(BF16)
            nm_out[a, :, part] = new_master
            nm1_out[a, :, part] = new1
            nm2_out[a, :, part] = new2
            nw_out[q, core, a, :, part] = new_master.astype(BF16)
        to_other_chips(p, nown, nw_out, N, recv_n)

    update(1, last_x(s_sx, s_rxz, S1))
    update(0, last_z(s_sz, s_rzx, S1))

    second_x(vpx, v_rx, v_sx, v_rxz, V1)
    second_z(vpz, v_rz, v_sz, v_rzx, V1)
    on_to_other_core(1, nw_out, N, recv_n)
    on_to_other_core(0, nw_out, N, recv_n)
    v_out[:, cols:] = last_x(v_sx, v_rxz, V1).astype(BF16)
    v_out[:, :cols] = last_z(v_sz, v_rzx, V1).astype(BF16)
    of_other_core(1, nw_out, N)
    of_other_core(0, nw_out, N)

    all_sent(wbuf, W)
    all_sent(nw_out, N)
    wait(send.at[GC], rc)
    wait(send.at[GQ], rq)
    for slot, (rz, rx, rzx, rxz) in (
        (S1, (s_rz, s_rx, s_rzx, s_rxz)),
        (V1, (v_rz, v_rx, v_rzx, v_rxz)),
    ):
        wait(send.at[slot], rz)
        wait(send.at[slot + 1], rx)
        wait(send.at[slot + 2], rzx)
        wait(send.at[slot + 3], rxz)


def hand_over(*refs):
    n = len(refs) // 2
    copies = [
        pltpu.make_async_copy(refs[i], refs[n + i], refs[-1].at[i]) for i in range(n)
    ]
    for copy in copies:
        copy.start()
    for copy in copies:
        copy.wait()


def body(x_long, dv_long, x_short, dv_short, long_len, short_len, master, moment1, moment2):
    kv = master.shape[2]
    cols = 5 * kv // 8
    rest = kv - cols
    rows_l, outer, inner = x_long.shape
    xl = jnp.transpose(x_long, (1, 2, 0)).reshape(outer, inner, rows_l // 128, 128)
    xl = jnp.transpose(xl, (0, 2, 1, 3)).reshape(-1, 128)
    xs = x_short.reshape(-1, x_short.shape[2])
    operands = (xl, dv_long, xs, dv_short, long_len, short_len, master, moment1, moment2)
    state = jax.ShapeDtypeStruct(master.shape, F32)
    outs = (
        jax.ShapeDtypeStruct((8, kv), BF16),
        state,
        state,
        state,
        jax.ShapeDtypeStruct((NQ, NC, 2, 4, kv), BF16),
    )
    vmem = pl.BlockSpec(memory_space=pltpu.VMEM)
    hbm = pl.BlockSpec(memory_space=pl.ANY)
    smem = pl.BlockSpec(memory_space=pltpu.SMEM)
    sums = [
        pltpu.VMEM((NZ - 1, NX, 8, cols), BF16),
        pltpu.VMEM((NX - 1, NZ, 8, rest), BF16),
        pltpu.VMEM((NX, 8, cols), BF16),
        pltpu.VMEM((NZ, 8, rest), BF16),
        pltpu.VMEM((NX - 1, 8, cols), BF16),
        pltpu.VMEM((NZ - 1, 8, rest), BF16),
    ]
    results = pl.pallas_call(
        kernel,
        out_shape=tuple(pltpu.VMEM(o.shape, o.dtype) for o in outs),
        in_specs=[hbm] * 4 + [smem] * 2 + [hbm] * 3,
        out_specs=(vmem,) * 5,
        scratch_shapes=[
            pltpu.VMEM(a.shape, a.dtype) for a in operands if a.dtype != jnp.int32
        ]
        + [
            pltpu.VMEM(xs.shape, F32),
            pltpu.VMEM((outer * inner, rows_l), BF16),
            pltpu.VMEM((NQ, NC, 8, kv), BF16),
            pltpu.VMEM((NZ, NX, 8, cols), BF16),
            pltpu.VMEM((NZ, NX, 8, rest), BF16),
            pltpu.VMEM((NZ, NX, 8, cols), BF16),
            pltpu.VMEM((NZ, NX, 8, rest), BF16),
            pltpu.VMEM((8, kv), BF16),
            pltpu.VMEM((NQ, NC, 8, kv), BF16),
            pltpu.VMEM((2, 4, kv), BF16),
            pltpu.VMEM((NQ, 8, kv), BF16),
            pltpu.VMEM((NQ, 8, kv), BF16),
            pltpu.VMEM((NQ - 1, 8, kv), BF16),
        ]
        + sums
        + sums
        + [
            pltpu.SemaphoreType.DMA((7,)),
            pltpu.SemaphoreType.DMA((18,)),
            pltpu.SemaphoreType.DMA((18,)),
            pltpu.SemaphoreType.DMA((2, NY)),
            pltpu.SemaphoreType.DMA((2, NY)),
        ],
        compiler_params=pltpu.CompilerParams(collective_id=0, has_side_effects=True),
    )(*operands)
    v, nm, nm1, nm2, nw = pl.pallas_call(
        hand_over,
        out_shape=outs,
        in_specs=[vmem] * 5,
        out_specs=(hbm,) * 5,
        scratch_shapes=[pltpu.SemaphoreType.DMA((5,))],
    )(*(pltpu.with_memory_space_constraint(r, pltpu.VMEM) for r in results))
    return v, nm, nm1, nm2, nw.reshape(NQ * NC * 2, 4, kv)


def solution(mesh):
    placed = (
        P("dp", None, "tensor"),
        P("dp", None),
        P("tensor", "dp", None),
        P("tensor", None),
        P("dp"),
        P("tensor"),
        P("dp", "tensor", None),
        P("dp", "tensor", None),
        P("dp", "tensor", None),
    )
    return jax.shard_map(
        body,
        mesh=mesh,
        in_specs=placed,
        out_specs=(
            P(("dp", "tensor"), None),
            P("dp", "tensor", None),
            P("dp", "tensor", None),
            P("dp", "tensor", None),
            P(None, "tensor", None),
        ),
        check_vma=False,
    )
```

```python
import jax
import jax.numpy as jnp
from jax import lax
from jax.experimental import pallas as pl
from jax.experimental.pallas import tpu as pltpu
from jax.sharding import PartitionSpec as P

MESH = pl.DeviceIdType.MESH
F32 = jnp.float32
BF16 = jnp.bfloat16

NZ, NX = 8, 4
NY, NC = 8, 2
NQ = 2 * NY
W, WF, N, NF, GC, GQ, S1, V1 = 0, 2, 4, 6, 8, 9, 10, 14


def contract(left, right, left_dim):
    return lax.dot_general(
        left, right, (((left_dim,), (0,)), ((), ())), preferred_element_type=F32
    )


def far_first(i):
    return (4 + (i + 1) // 2 * (2 * (i % 2) - 1)) % 8


def loop(n, f):
    for i in range(n):
        f(i)


def swap_quads(even, odd):
    low = lax.broadcasted_iota(jnp.int32, even.shape, 1) < 4
    return (
        jnp.where(low, even, pltpu.roll(odd, 4, 1)),
        jnp.where(low, pltpu.roll(even, 4, 1), odd),
    )


def kernel(
    xl_hbm, dvl_hbm, xs_hbm, dvs_hbm, llen_ref, slen_ref, m_hbm, m1_hbm, m2_hbm,
    v_out, nm_out, nm1_out, nm2_out, nw_out,
    xl_ref, dvl_ref, xs_ref, dvs_ref, m_ref, m1_ref, m2_ref,
    xsf, xt, gl, gsz, gsx, vpz, vpx, wown, wbuf, nown,
    rc, c1, rq,
    s_rz, s_rx, s_sz, s_sx, s_rzx, s_rxz,
    v_rz, v_rx, v_sz, v_sx, v_rzx, v_rxz,
    load, send, recv, recv_w, recv_n,
):
    dp = lax.axis_index("dp")
    tensor = lax.axis_index("tensor")
    q, core = dp // NC, lax.rem(dp, NC)
    z, xh = tensor // NX, lax.rem(tensor, NX)
    xl, y = q // NY, lax.rem(q, NY)
    kv = v_out.shape[1]
    cols = v_sz.shape[2]

    def to_z(k):
        return lax.rem(z + k, NZ)

    def to_x(k):
        return lax.rem(xh + k, NX)

    def at_z(k):
        return (dp, to_z(k) * NX + xh)

    def at_x(k):
        return (dp, z * NX + to_x(k))

    def at_q(p):
        return (p * NC + core, tensor)

    def step_q(i):
        far = far_first(i // 2)
        side = (xl if i % 2 else 1 - xl) * NY
        return side + lax.rem(y + far, NY), side + lax.rem(y - far + NY, NY)

    other = (q * NC + (1 - core), tensor)
    barrier = pltpu.get_barrier_semaphore()

    def greet(device):
        pl.semaphore_signal(barrier, inc=1, device_id=device, device_id_type=MESH)

    loop(NQ - 1, lambda i: greet(at_q(step_q(i)[0])))
    loop(NZ - 1, lambda i: greet(at_z(far_first(i))))
    loop(NX - 1, lambda i: greet(at_x(i + 1)))
    greet(other)

    loads = [
        pltpu.make_async_copy(src, dst, load.at[i])
        for i, (src, dst) in enumerate((
            (xs_hbm, xs_ref), (dvs_hbm, dvs_ref), (m_hbm, m_ref),
            (xl_hbm, xl_ref), (dvl_hbm, dvl_ref),
            (m1_hbm, m1_ref), (m2_hbm, m2_ref),
        ))
    ]
    for copy in loads:
        copy.start()

    def remote(src, dst, slot, device, arrival=None):
        pltpu.make_async_remote_copy(
            src_ref=src, dst_ref=dst, send_sem=send.at[slot],
            recv_sem=recv.at[slot] if arrival is None else arrival,
            device_id=device, device_id_type=MESH,
        ).start()

    def wait(sem, ref):
        pltpu.make_async_copy(ref, ref, sem).wait()

    parts = (slice(0, cols), slice(cols, kv))

    def to_other_chips(p, own, gathered, slot, arrivals):
        mine = own.at[..., parts[p]]
        there = gathered.at[q, core].at[..., parts[p]]
        remote(mine, there, slot + 2 + p, other)
        loop(
            NQ - 1,
            lambda i: remote(
                mine, there, slot + p, at_q(step_q(i)[0]), arrivals.at[p, i // 2]
            ),
        )

    def on_to_other_core(p, gathered, slot, arrivals):
        for pair in range(NY):
            steps = range(2 * pair, min(2 * pair + 2, NQ - 1))
            arrived = gathered.at[pl.ds(0, len(steps)), core]
            wait(arrivals.at[p, pair], arrived.at[..., parts[p]])
            for i in steps:
                chunk = gathered.at[step_q(i)[1], core].at[..., parts[p]]
                remote(chunk, chunk, slot + 2 + p, other)

    def of_other_core(p, gathered, slot):
        wait(recv.at[slot + 2 + p], gathered.at[:, 1 - core].at[..., parts[p]])

    def all_sent(gathered, slot):
        for p in range(2):
            sent = gathered.at[pl.ds(0, NQ - 1), core]
            wait(send.at[slot + p], sent.at[..., parts[p]])
            wait(send.at[slot + 2 + p], gathered.at[:, core].at[..., parts[p]])

    def first_z(part, rz, slot):
        for i in range(NZ - 1):
            k = far_first(i)
            remote(part.at[to_z(k)], rz.at[k - 1], slot, at_z(k))

    def first_x(part, rx, slot):
        for k in (2, 1, 3):
            remote(part.at[:, to_x(k)], rx.at[k - 1], slot + 1, at_x(k))

    def second_z(part, rz, sz, rzx, slot):
        wait(recv.at[slot], rz)
        total = part[z].astype(F32)
        for k in range(NZ - 1):
            total += rz[k].astype(F32)
        sz[...] = total.astype(BF16)
        for k in (2, 1, 3):
            remote(sz.at[to_x(k)], rzx.at[k - 1], slot + 2, at_x(k))

    def second_x(part, rx, sx, rxz, slot):
        wait(recv.at[slot + 1], rx)
        total = part[:, xh].astype(F32)
        for k in range(NX - 1):
            total += rx[k].astype(F32)
        sx[...] = total.astype(BF16)
        for i in range(NZ - 1):
            k = far_first(i)
            remote(sx.at[to_z(k)], rxz.at[k - 1], slot + 3, at_z(k))

    def last_z(sz, rzx, slot):
        wait(recv.at[slot + 2], rzx)
        total = sz[xh].astype(F32)
        for k in range(NX - 1):
            total += rzx[k].astype(F32)
        return total

    def last_x(sx, rxz, slot):
        wait(recv.at[slot + 3], rxz)
        total = sx[z].astype(F32)
        for k in range(NZ - 1):
            total += rxz[k].astype(F32)
        return total

    loads[0].wait()
    xsf[...] = xs_ref[...].astype(F32)
    rows = xs_ref.shape[0] // 2
    live = lax.broadcasted_iota(jnp.int32, (rows, xs_ref.shape[1]), 0) < slen_ref[0]
    x0 = jnp.where(live, xsf[pl.ds(0, rows, stride=2), :], 0.0).astype(BF16)
    x1 = jnp.where(live, xsf[pl.ds(1, rows, stride=2), :], 0.0).astype(BF16)
    loads[1].wait()
    dvs = dvs_ref[...]
    g0 = contract(x0, dvs, 0).reshape(16, 8, kv)
    g1 = contract(x1, dvs, 0).reshape(16, 8, kv)
    for s, owners in enumerate(swap_quads(g0, g1)):
        owners = owners.astype(BF16).reshape(NZ, 2, 8, kv)
        for p in range(2):
            gsz[:, 2 * p + s] = owners[:, p, :, :cols]
            gsx[:, 2 * p + s] = owners[:, p, :, cols:]

    loads[2].wait()
    w = jnp.concatenate([m_ref[0], m_ref[1]], axis=0).astype(BF16)
    wown[...] = w
    wbuf[q, core] = w

    loads[3].wait()
    quads = xl_ref[...].astype(F32).reshape(32, 2, 8, 128)
    blocks = swap_quads(quads[:, 0], quads[:, 1])
    x = jnp.concatenate([b.reshape(256, 128) for b in blocks], axis=1)
    live = lax.broadcasted_iota(jnp.int32, x.shape, 1) < llen_ref[0]
    x = jnp.where(live, x, 0.0).astype(BF16)
    xt[...] = x
    loads[4].wait()
    gl[...] = contract(x, dvl_ref[...], 1).astype(BF16).reshape(gl.shape)

    pl.semaphore_wait(barrier, NZ - 1 + NX - 1 + NQ - 1 + 1)
    remote(gl.at[:, 1 - core], rc, GC, other)
    to_other_chips(0, wown, wbuf, W, recv_w)
    first_z(gsz, s_rz, S1)
    first_x(gsx, s_rx, S1)
    to_other_chips(1, wown, wbuf, W, recv_w)

    wait(recv.at[GC], rc)

    def add(i, c):
        c1[i] = (gl[i, core].astype(F32) + rc[i].astype(F32)).astype(BF16)
        return c

    lax.fori_loop(0, NQ, add, 0)

    on_to_other_core(0, wbuf, W, recv_w)
    for i in range(NQ - 1):
        to = step_q(i)[0]
        remote(c1.at[to], rq.at[i], GQ, at_q(to))

    second_x(gsx, s_rx, s_sx, s_rxz, S1)
    of_other_core(0, wbuf, W)
    weights = wbuf[:, :, :, :cols].reshape(NQ * NC * 8, cols)
    vpz[...] = contract(xt[...], weights, 0).astype(BF16).reshape(vpz.shape)
    first_z(vpz, v_rz, V1)

    second_z(gsz, s_rz, s_sz, s_rzx, S1)
    on_to_other_core(1, wbuf, W, recv_w)
    of_other_core(1, wbuf, W)
    weights = wbuf[:, :, :, cols:].reshape(NQ * NC * 8, kv - cols)
    vpx[...] = contract(xt[...], weights, 0).astype(BF16).reshape(vpx.shape)
    first_x(vpx, v_rx, V1)

    loads[5].wait()
    loads[6].wait()
    wait(recv.at[GQ], rq)
    first_corr = 1.0 - 0.9**10
    second_corr = 1.0 - 0.999**10

    def update(p, short):
        part = parts[p]
        grad = short + c1[q, :, part].astype(F32)
        for k in range(NQ - 1):
            grad += rq[k, :, part].astype(F32)
        for a in range(2):
            ga = grad[4 * a : 4 * a + 4]
            master = m_ref[a, :, part]
            new1 = 0.9 * m1_ref[a, :, part] + 0.1 * ga
            new2 = 0.999 * m2_ref[a, :, part] + 0.001 * ga * ga
            step = new1 / first_corr / (jnp.sqrt(new2 / second_corr) + 1e-08)
            new_master = master - 0.01 * (step + 0.1 * master)
            nown[a, :, part] = new_master.astype(BF16)
            nm_out[a, :, part] = new_master
            nm1_out[a, :, part] = new1
            nm2_out[a, :, part] = new2
            nw_out[q, core, a, :, part] = new_master.astype(BF16)
        to_other_chips(p, nown, nw_out, N, recv_n)

    update(1, last_x(s_sx, s_rxz, S1))
    update(0, last_z(s_sz, s_rzx, S1))

    second_x(vpx, v_rx, v_sx, v_rxz, V1)
    second_z(vpz, v_rz, v_sz, v_rzx, V1)
    on_to_other_core(1, nw_out, N, recv_n)
    on_to_other_core(0, nw_out, N, recv_n)
    v_out[:, cols:] = last_x(v_sx, v_rxz, V1).astype(BF16)
    v_out[:, :cols] = last_z(v_sz, v_rzx, V1).astype(BF16)
    of_other_core(1, nw_out, N)
    of_other_core(0, nw_out, N)

    all_sent(wbuf, W)
    all_sent(nw_out, N)
    wait(send.at[GC], rc)
    wait(send.at[GQ], rq)
    for slot, (rz, rx, rzx, rxz) in (
        (S1, (s_rz, s_rx, s_rzx, s_rxz)),
        (V1, (v_rz, v_rx, v_rzx, v_rxz)),
    ):
        wait(send.at[slot], rz)
        wait(send.at[slot + 1], rx)
        wait(send.at[slot + 2], rzx)
        wait(send.at[slot + 3], rxz)


def hand_over(*refs):
    n = len(refs) // 2
    copies = [
        pltpu.make_async_copy(refs[i], refs[n + i], refs[-1].at[i]) for i in range(n)
    ]
    for copy in copies:
        copy.start()
    for copy in copies:
        copy.wait()


def body(x_long, dv_long, x_short, dv_short, long_len, short_len, master, moment1, moment2):
    kv = master.shape[2]
    cols = 5 * kv // 8
    rest = kv - cols
    rows_l, outer, inner = x_long.shape
    xl = jnp.transpose(x_long, (1, 2, 0)).reshape(outer, inner, rows_l // 128, 128)
    xl = jnp.transpose(xl, (0, 2, 1, 3)).reshape(-1, 128)
    xs = x_short.reshape(-1, x_short.shape[2])
    operands = (xl, dv_long, xs, dv_short, long_len, short_len, master, moment1, moment2)
    state = jax.ShapeDtypeStruct(master.shape, F32)
    outs = (
        jax.ShapeDtypeStruct((8, kv), BF16),
        state,
        state,
        state,
        jax.ShapeDtypeStruct((NQ, NC, 2, 4, kv), BF16),
    )
    vmem = pl.BlockSpec(memory_space=pltpu.VMEM)
    hbm = pl.BlockSpec(memory_space=pl.ANY)
    smem = pl.BlockSpec(memory_space=pltpu.SMEM)
    sums = [
        pltpu.VMEM((NZ - 1, NX, 8, cols), BF16),
        pltpu.VMEM((NX - 1, NZ, 8, rest), BF16),
        pltpu.VMEM((NX, 8, cols), BF16),
        pltpu.VMEM((NZ, 8, rest), BF16),
        pltpu.VMEM((NX - 1, 8, cols), BF16),
        pltpu.VMEM((NZ - 1, 8, rest), BF16),
    ]
    results = pl.pallas_call(
        kernel,
        out_shape=tuple(pltpu.VMEM(o.shape, o.dtype) for o in outs),
        in_specs=[hbm] * 4 + [smem] * 2 + [hbm] * 3,
        out_specs=(vmem,) * 5,
        scratch_shapes=[
            pltpu.VMEM(a.shape, a.dtype) for a in operands if a.dtype != jnp.int32
        ]
        + [
            pltpu.VMEM(xs.shape, F32),
            pltpu.VMEM((outer * inner, rows_l), BF16),
            pltpu.VMEM((NQ, NC, 8, kv), BF16),
            pltpu.VMEM((NZ, NX, 8, cols), BF16),
            pltpu.VMEM((NZ, NX, 8, rest), BF16),
            pltpu.VMEM((NZ, NX, 8, cols), BF16),
            pltpu.VMEM((NZ, NX, 8, rest), BF16),
            pltpu.VMEM((8, kv), BF16),
            pltpu.VMEM((NQ, NC, 8, kv), BF16),
            pltpu.VMEM((2, 4, kv), BF16),
            pltpu.VMEM((NQ, 8, kv), BF16),
            pltpu.VMEM((NQ, 8, kv), BF16),
            pltpu.VMEM((NQ - 1, 8, kv), BF16),
        ]
        + sums
        + sums
        + [
            pltpu.SemaphoreType.DMA((7,)),
            pltpu.SemaphoreType.DMA((18,)),
            pltpu.SemaphoreType.DMA((18,)),
            pltpu.SemaphoreType.DMA((2, NY)),
            pltpu.SemaphoreType.DMA((2, NY)),
        ],
        compiler_params=pltpu.CompilerParams(collective_id=0, has_side_effects=True),
    )(*operands)
    v, nm, nm1, nm2, nw = pl.pallas_call(
        hand_over,
        out_shape=outs,
        in_specs=[vmem] * 5,
        out_specs=(hbm,) * 5,
        scratch_shapes=[pltpu.SemaphoreType.DMA((5,))],
    )(*(pltpu.with_memory_space_constraint(r, pltpu.VMEM) for r in results))
    return v, nm, nm1, nm2, nw.reshape(NQ * NC * 2, 4, kv)


def solution(mesh):
    placed = (
        P("dp", None, "tensor"),
        P("dp", None),
        P("tensor", "dp", None),
        P("tensor", None),
        P("dp"),
        P("tensor"),
        P("dp", "tensor", None),
        P("dp", "tensor", None),
        P("dp", "tensor", None),
    )
    return jax.shard_map(
        body,
        mesh=mesh,
        in_specs=placed,
        out_specs=(
            P(("dp", "tensor"), None),
            P("dp", "tensor", None),
            P("dp", "tensor", None),
            P("dp", "tensor", None),
            P(None, "tensor", None),
        ),
        check_vma=False,
    )
```
